512 devices in a mesh: ctx: 64 (over z_lo, y, x), head: 8 (over z_hi, core).
Axes of the slice: x: 4, y: 8, z: 8 (z_hi: 4, z_lo: 2; z = z_hi * 2 + z_lo), core: 2. Of those that a mesh axis runs over, the one named last changes fastest.
Arguments:
- queries: bfloat16 [8192, 2048], P('ctx', 'head'), may hold values from -6 to 6
- key_rows: bfloat16 [8192, 128], P('ctx'), may hold values from -6 to 6
- value_rows: bfloat16 [8192, 128], P('ctx'), may hold values from -6 to 6
- out_grad: bfloat16 [8192, 2048], P('ctx', 'head'), may hold values from -6 to 6
- doc_lengths: int32 [8], replicated, may hold values from 1 to 4096, 8192 in all
- span_order: int32 [64, 2], replicated, may hold values from 0 to 127, as said below
Outputs:
- query_grad: bfloat16 [8192, 2048], P('ctx', 'head')
- key_grad: bfloat16 [8192, 128], P(('ctx', 'head'))
- value_grad: bfloat16 [8192, 128], P(('ctx', 'head'))
The draws below stay inside these ranges and needn't reach their ends.
Inputs may be any that keep to these rules, and one draw needn't show every extreme that they name: `doc_lengths`: the lengths sum to 8192; the longest is exactly 4096. `span_order`: row i holds a span number c and its mirror 128 - 1 - c, in that order; the first entries of all rows are distinct.
All inputs are finite; a program needn't handle non-finite values.
Results may differ from the reference program's by a relative error of at most 0.025.
Values may be sent and summed in bfloat16 or wider, within the bound.
A program may use at most 64 MiB of HBM per device.

```python
import math
import jax
import jax.numpy as jnp
import numpy as np
from jax import lax

HD = 128
QHEADS = 16
NDOCS = 8
SPAN = 64
NCHUNK = 128
TOKENS = 8192


def draw_queries(key, part):
    width = QHEADS * HD
    base = jnp.clip(jax.random.normal(jax.random.fold_in(key, 14), (TOKENS, width), jnp.float32), -6.0, 6.0)
    return base.astype(jnp.bfloat16)


def draw_key_rows(key, part):
    base = jnp.clip(jax.random.normal(jax.random.fold_in(key, 24), (TOKENS, HD), jnp.float32), -6.0, 6.0)
    return base.astype(jnp.bfloat16)


def draw_span_order(key, part):
    first = jax.random.permutation(jax.random.fold_in(key, 31), NCHUNK // 2)
    return jnp.stack([first, NCHUNK - 1 - first], axis=1).astype(jnp.int32)


def block_levels(rng, extent, shards, least, high):
    def one(axis_at, parts):
        draws = jax.random.uniform(jax.random.fold_in(jax.random.fold_in(rng, 6), axis_at), (parts,), jnp.float32, least / len(shards), high / len(shards))
        return jnp.repeat(jnp.exp(draws), extent[axis_at] // parts).reshape((-1,) + (1,) * (len(extent) - axis_at - 1))

    loudness = one(*shards[0])
    for cut in shards[1:]:
        loudness = loudness * one(*cut)
    return loudness


def length_profile(count, total, bound, lean):
    portions = [(1 << 20) // math.isqrt(standing ** lean) + 1 for standing in range(2, count + 1)]
    surplus, given = total - bound - (count - 1), [1] * (count - 1)
    while surplus > 0:
        free = [i for i in range(count - 1) if given[i] < bound]
        whole, budget = sum([portions[i] for i in free]), surplus
        for i in free:
            more = min(bound - given[i], max(1, budget * portions[i] // whole), surplus)
            given[i] = given[i] + more
            surplus = surplus - more
    return np.array([bound] + given)


def ragged_sizes(stream_key, amount, total, bound, lean):
    if amount == 2:
        one = jax.random.randint(stream_key, (), max(1, total - bound), min(bound, total - 1) + 1)
        return jnp.stack([one, total - one])
    lengths = jnp.asarray(length_profile(amount, total, bound, lean), jnp.int32)
    pairs = (amount - 1) // 2
    giver, receiver = lengths[1:1 + 2 * pairs:2], lengths[2:2 + 2 * pairs:2]
    room = jnp.minimum(giver - 1, bound - receiver)
    passed = jax.random.randint(jax.random.fold_in(stream_key, 1), (pairs,), 0, 1 << 20) % (room + 1)
    lengths = lengths.at[1:1 + 2 * pairs:2].set(giver - passed).at[2:2 + 2 * pairs:2].set(receiver + passed)
    return lengths[jax.random.permutation(jax.random.fold_in(stream_key, 2), amount)]


def scatter_about(rng, extent, scale, reach, cuts=(), held_as=jnp.bfloat16):
    result = jax.random.normal(rng, extent, jnp.float32) * scale
    if len(cuts) > 0:
        result = block_levels(rng, extent, cuts, -0.22, 0.18) * result
    return jnp.clip(result, min=-reach, max=reach).astype(held_as)


def setup_inputs(seed: int = 0) -> dict:
    keys = jax.random.split(jax.random.key(seed), 7)
    return {
        "queries": draw_queries(jax.random.fold_in(keys[6], 71), 0),
        "key_rows": draw_key_rows(jax.random.fold_in(keys[6], 71), 0),
        "value_rows": scatter_about(keys[2], (TOKENS, HD), 1.0, 6.0, ((0, 64),)),
        "out_grad": scatter_about(keys[3], (TOKENS, QHEADS * HD), 1.0, 6.0, ((0, 64), (1, 8))),
        "doc_lengths": ragged_sizes(keys[4], NDOCS, TOKENS, TOKENS // 2, 2).astype(jnp.int32),
        "span_order": draw_span_order(jax.random.fold_in(keys[6], 71), 0),
    }


def reference(queries, key_rows, value_rows, out_grad, doc_lengths, span_order):
    scaling = HD ** -0.5
    positions = (span_order.reshape(-1)[:, None] * SPAN + jnp.arange(SPAN, dtype=jnp.int32)[None, :]).reshape(-1).astype(jnp.int32)
    starts = jnp.cumsum(doc_lengths) - doc_lengths
    documents = jnp.sum((starts[None, :] <= positions[:, None]).astype(jnp.int32), axis=1) - 1
    keys_wide = key_rows.astype(jnp.float32)
    values_wide = value_rows.astype(jnp.float32)
    block_rows = min(256, TOKENS)
    block_count = TOKENS // block_rows
    query_blocks = queries.reshape(block_count, block_rows, QHEADS, HD)
    grad_blocks = out_grad.reshape(block_count, block_rows, QHEADS, HD)
    pos_blocks = positions.reshape(block_count, block_rows)
    doc_blocks = documents.reshape(block_count, block_rows)

    def one_block(carry, inputs):
        key_total, value_total = carry
        query_block, grad_block, pos_block, doc_block = inputs
        query_wide = query_block.astype(jnp.float32)
        grad_wide = grad_block.astype(jnp.float32)
        scores = jnp.einsum("qhd,kd->hqk", query_wide, keys_wide) * scaling
        allowed = (doc_block[:, None] == documents[None, :]) & (positions[None, :] <= pos_block[:, None])
        masked = jnp.where(allowed[None], scores, -1e30)
        row_max = jnp.max(masked, axis=-1, keepdims=True)
        row_total = jnp.sum(jnp.where(allowed[None], jnp.exp(masked - row_max), 0.0), axis=-1, keepdims=True)
        log_total = row_max + jnp.log(row_total)
        weights = jnp.where(allowed[None], jnp.exp(masked - log_total), 0.0)
        dprobs = jnp.einsum("qhd,kd->hqk", grad_wide, values_wide)
        row_delta = jnp.sum(weights * dprobs, axis=-1, keepdims=True)
        weights_low = weights.astype(jnp.bfloat16)
        dscores = (weights * (dprobs - row_delta)).astype(jnp.bfloat16)
        value_total = value_total + jnp.einsum("hqk,qhd->kd", weights_low.astype(jnp.float32), grad_wide)
        key_total = key_total + jnp.einsum("hqk,qhd->kd", dscores.astype(jnp.float32), query_wide) * scaling
        query_grad = (jnp.einsum("hqk,kd->qhd", dscores.astype(jnp.float32), keys_wide) * scaling).astype(jnp.bfloat16)
        return (key_total, value_total), query_grad

    zeros = jnp.zeros((TOKENS, HD), jnp.float32)
    (key_total, value_total), query_grad = lax.scan(one_block, (zeros, zeros), (query_blocks, grad_blocks, pos_blocks, doc_blocks))
    return query_grad.reshape(TOKENS, QHEADS * HD), key_total.astype(jnp.bfloat16), value_total.astype(jnp.bfloat16)
```

```python
import functools
import math

import jax
import jax.numpy as jnp
from jax import lax
from jax.experimental import pallas as pl
from jax.experimental.pallas import tpu as pltpu
from jax.sharding import PartitionSpec as P

MESH = pl.DeviceIdType.MESH
F32 = jnp.float32
BF16 = jnp.bfloat16
NX, NY, NZH = 4, 8, 4
HD = 128
NEG = -1e30
SCALE = HD ** -0.5
EXP_SCALE = SCALE / math.log(2.0)
CK = 512
UQ = 256


def kernel(
    lens_ref, order_ref, q_ref, g_ref, k_ref, v_ref,
    dq_ref, dk_ref, dv_ref,
    kv, qa, ga, qs, gs, kp, qlim, es, dps, ws, dss, dqa, pf, st, rst, lim,
    dqb, dqr, sb, m1, rr, rl, yb, yr, zb, zr,
    lsem, qsend, qrecv, ysend, yrecv, xsend, xrecv, ssend, srecv, dsend, drecv,
    m1send, m1recv, rsend, rrecv, lsend, lrecv, rysend, ryrecv, zsend, zrecv,
):
    ctx = lax.axis_index("ctx")
    head = lax.axis_index("head")
    zl, y, x = ctx // 32, (ctx // 4) % 8, ctx % 4
    zh, core = head // 2, head % 2

    def at(zl_, y_, x_):
        return zl_ * 32 + y_ * 4 + x_

    right = (at(zl, y, (x + 1) % 4), head)
    left = (at(zl, y, (x + 3) % 4), head)
    ydev = [(at(zl, (y + r) % 8, x), head) for r in range(8)]
    zdev = [(ctx, ((zh + r) % 4) * 2 + core) for r in range(4)]
    gdev = [
        (at((zl + k // 2) % 2, y, x), zh * 2 + (core + k % 2) % 2) for k in range(4)
    ]

    stage = [
        pltpu.make_async_copy(k_ref.at[:, core], kv.at[0, x, y], lsem.at[0]),
        pltpu.make_async_copy(v_ref.at[:, core], kv.at[1, x, y], lsem.at[1]),
        pltpu.make_async_copy(q_ref, qa.at[0], lsem.at[2]),
        pltpu.make_async_copy(g_ref, ga.at[0], lsem.at[3]),
    ]
    for c in stage:
        c.start()

    barrier = pltpu.get_barrier_semaphore()
    peers = [right, left] + ydev[1:] + zdev[1:] + gdev[1:]
    for p in peers:
        pl.semaphore_signal(barrier, inc=1, device_id=p, device_id_type=MESH)
    pl.semaphore_wait(barrier, len(peers))

    pending = []

    def send(src, dst, ss, rs, dev):
        c = pltpu.make_async_remote_copy(
            src_ref=src, dst_ref=dst, send_sem=ss, recv_sem=rs,
            device_id=dev, device_id_type=MESH,
        )
        c.start()
        pending.append(c)
        return c

    def arrival(dst, ss, rs):
        return pltpu.make_async_remote_copy(
            src_ref=dst, dst_ref=dst, send_sem=ss, recv_sem=rs,
            device_id=right, device_id_type=MESH,
        )

    stage[0].wait()
    stage[1].wait()

    def blk(xr, yr_):
        return kv.at[:, (x + xr) % 4, (y + yr_) % 8]

    def x_forward(r):
        b = blk(0, r)
        send(b, b, xsend.at[r, 0], xrecv.at[r, 0], right)
        send(b, b, xsend.at[r, 1], xrecv.at[r, 1], left)

    def y_send(r, up):
        b = blk(0, r)
        i = (-r) % 8 if up else r
        j = i if up else 4 + i
        dev = ydev[1] if up else ydev[7]
        send(b, b, ysend.at[j], yrecv.at[j], dev)

    y_send(0, True)
    y_send(0, False)
    x_forward(0)
    for k in range(1, 4):
        send(q_ref, qa.at[k], qsend.at[k, 0], qrecv.at[k, 0], gdev[k])
        send(g_ref, ga.at[k], qsend.at[k, 1], qrecv.at[k, 1], gdev[k])

    def x_arrive(r):
        bl, br = blk(3, r), blk(1, r)
        arrival(bl, xsend.at[r, 0], xrecv.at[r, 0]).wait_recv()
        if r % 2 == 0:
            send(bl, bl, xsend.at[r, 2], xrecv.at[r, 2], right)
        arrival(br, xsend.at[r, 1], xrecv.at[r, 1]).wait_recv()
        if r % 2 == 1:
            send(br, br, xsend.at[r, 2], xrecv.at[r, 2], left)

    prev = [0]
    for d in range(1, 5):
        r = -d
        b = blk(0, r)
        arrival(b, ysend.at[d - 1], yrecv.at[d - 1]).wait_recv()
        if d < 4:
            y_send(r, True)
        x_forward(r % 8)
        got = [r % 8]
        if d < 4:
            r = d
            b = blk(0, r)
            arrival(b, ysend.at[3 + d], yrecv.at[3 + d]).wait_recv()
            if d < 3:
                y_send(r, False)
            x_forward(r)
            got.append(r)
        for p in prev:
            x_arrive(p)
        prev = got
    for p in prev:
        x_arrive(p)
    for r in range(8):
        b = blk(2, r)
        arrival(b, xsend.at[r, 2], xrecv.at[r, 2]).wait_recv()

    stage[2].wait()
    stage[3].wait()
    for k in range(1, 4):
        arrival(qa.at[k], qsend.at[k, 0], qrecv.at[k, 0]).wait_recv()
        arrival(ga.at[k], qsend.at[k, 1], qrecv.at[k, 1]).wait_recv()
    lane = lax.broadcasted_iota(jnp.int32, (8, HD), 1) % 64
    starts = []
    total = jnp.int32(0)
    for i in range(8):
        starts.append(total)
        total = total + lens_ref[i]
    for dz in range(2):
        octx = at((zl + dz) % 2, y, x)
        for h in range(2):
            u = dz * 2 + h
            for dc in range(2):
                for hd in range(2):
                    rows = slice(h * 64, h * 64 + 64)
                    cols = slice(hd * HD, hd * HD + HD)
                    o = (dc * 2 + hd) * 64
                    qs[u, o : o + 64, :] = qa[dz * 2 + dc, rows, cols]
                    gs[u, o : o + 64, :] = ga[dz * 2 + dc, rows, cols]
            qp = order_ref[octx, h] * 64 + lane
            first = jnp.zeros_like(qp)
            for s in starts:
                first = jnp.maximum(first, jnp.where(qp >= s, s, 0))
            qlim[u, 0] = qp
            qlim[u, 1] = first
    row = lax.broadcasted_iota(jnp.int32, (32, HD), 0)
    pattern = (row // 16) * 32 + row % 16 + core * 16
    for xc in range(4):
        for yc in range(8):
            for h in range(2):
                span = order_ref[at(zl, yc, xc), h]
                o = yc * 64 + h * 32
                kp[xc, o : o + 32, :] = pattern + span * 64

    def pass1(i, carry):
        xc, u = i // 4, i % 4
        keys = kv[0, xc].reshape(CK, HD)
        vals = kv[1, xc].reshape(CK, HD)
        dims = (((1,), (1,)), ((), ()))
        s = lax.dot_general(keys, qs[u], dims, preferred_element_type=F32)
        dp = lax.dot_general(vals, gs[u], dims, preferred_element_type=F32)
        dps[xc, u] = dp
        pos = kp[xc]
        allowed = (pos <= qlim[u, 0, 0:1, :]) & (pos >= qlim[u, 1, 0:1, :])
        for dc in range(2):
            cols = slice(dc * HD, dc * HD + HD)
            sh = jnp.where(allowed, s[:, cols], NEG)
            m = jnp.max(sh, axis=0, keepdims=True)
            e = jnp.exp2((sh - m) * EXP_SCALE)
            es[xc, u, :, cols] = e
            lim[xc, u, 0, 0:1, cols] = m
            lim[xc, u, 1, 0:1, cols] = jnp.sum(e, axis=0, keepdims=True)
            lim[xc, u, 2, 0:1, cols] = jnp.sum(e * dp[:, cols], axis=0, keepdims=True)
        return carry

    lax.fori_loop(0, 16, pass1, 0)

    for dz in range(2):
        for h in range(2):
            u = dz * 2 + h
            for dc in range(2):
                cols = slice(dc * HD, dc * HD + HD)
                ms = [lim[xc, u, 0, 0:1, cols] for xc in range(4)]
                m = jnp.maximum(jnp.maximum(ms[0], ms[1]), jnp.maximum(ms[2], ms[3]))
                sc = [jnp.exp2((a - m) * EXP_SCALE) for a in ms]
                k = dz * 2 + dc
                st[0, k, h : h + 1, :] = m
                st[1, k, h : h + 1, :] = sum(sc[c] * lim[c, u, 1, 0:1, cols] for c in range(4))
                st[2, k, h : h + 1, :] = sum(sc[c] * lim[c, u, 2, 0:1, cols] for c in range(4))
    for k in range(1, 4):
        send(st, rst.at[k], ssend.at[k], srecv.at[k], gdev[k])
    for k in range(1, 4):
        arrival(rst.at[k], ssend.at[k], srecv.at[k]).wait_recv()
    for k in range(4):
        ms = [st[0, k]] + [rst[p, 0, k ^ p] for p in range(1, 4)]
        ls = [st[1, k]] + [rst[p, 1, k ^ p] for p in range(1, 4)]
        ds = [st[2, k]] + [rst[p, 2, k ^ p] for p in range(1, 4)]
        m = jnp.maximum(jnp.maximum(ms[0], ms[1]), jnp.maximum(ms[2], ms[3]))
        sc = [jnp.exp2((a - m) * EXP_SCALE) for a in ms]
        inv = 1.0 / (sc[0] * ls[0] + sc[1] * ls[1] + sc[2] * ls[2] + sc[3] * ls[3])
        delta = (sc[0] * ds[0] + sc[1] * ds[1] + sc[2] * ds[2] + sc[3] * ds[3]) * inv
        dz, dc = k // 2, k % 2
        cols = slice(dc * HD, dc * HD + HD)
        for h in range(2):
            u = dz * 2 + h
            for xc in range(4):
                a = jnp.exp2((lim[xc, u, 0, 0:1, cols] - m[h : h + 1, :]) * EXP_SCALE)
                lim[xc, u, 3, 0:1, cols] = a * inv[h : h + 1, :]
            lim[0, u, 4, 0:1, cols] = delta[h : h + 1, :]

    dqa[...] = jnp.zeros_like(dqa)

    def column(c):
        xc = (x + c) % 4

        def unit(u, carry):
            w = es[xc, u] * lim[xc, u, 3, 0:1, :]
            o = pl.multiple_of(u * UQ, UQ)
            ws[:, pl.ds(o, UQ)] = w.astype(BF16)
            dss[:, pl.ds(o, UQ)] = (w * (dps[xc, u] - lim[0, u, 4, 0:1, :])).astype(BF16)
            return carry

        lax.fori_loop(0, 4, unit, 0)
        dims = (((1,), (0,)), ((), ()))
        q_all = qs[...].reshape(4 * UQ, HD)
        g_all = gs[...].reshape(4 * UQ, HD)
        dkc = lax.dot_general(dss[...], q_all, dims, preferred_element_type=F32)
        pf[c, 0] = dkc.reshape(8, 64, HD)
        dvc = lax.dot_general(ws[...], g_all, dims, preferred_element_type=F32)
        pf[c, 1] = dvc.reshape(8, 64, HD)
        keys = kv[0, xc].reshape(CK, HD)
        dqa[...] += lax.dot_general(
            dss[...], keys, (((0,), (0,)), ((), ())), preferred_element_type=F32
        )

    def mine(c, r):
        return pf[c, :, (y + r) % 8]

    order = [4, 3, 5, 2, 6, 1, 7, 0]
    column(2)
    for r in order:
        sb[2, r] = mine(2, r).astype(BF16)
        dev = right if r % 2 == 0 else left
        send(sb.at[2, r], m1.at[r], m1send.at[r], m1recv.at[r], dev)
    column(1)
    for r in order:
        if r % 2 == 1:
            sb[1, r] = mine(1, r).astype(BF16)
            send(sb.at[1, r], rr.at[r], rsend.at[r], rrecv.at[r], right)
    column(3)
    for r in order:
        if r % 2 == 0:
            sb[3, r] = mine(3, r).astype(BF16)
            send(sb.at[3, r], rl.at[r], lsend.at[r], lrecv.at[r], left)
    for r in order:
        arrival(m1.at[r], m1send.at[r], m1recv.at[r]).wait_recv()
        c = 1 if r % 2 == 0 else 3
        sb[c, r] = (mine(c, r) + m1[r].astype(F32)).astype(BF16)
        if r % 2 == 0:
            send(sb.at[1, r], rr.at[r], rsend.at[r], rrecv.at[r], right)
        else:
            send(sb.at[3, r], rl.at[r], lsend.at[r], lrecv.at[r], left)
    column(0)

    for k in range(4):
        dz, dc = k // 2, k % 2
        for h in range(2):
            for hd in range(2):
                o = (dz * 2 + h) * UQ + (dc * 2 + hd) * 64
                rows = slice(h * 64, h * 64 + 64)
                cols = slice(hd * HD, hd * HD + HD)
                part = dqa[o : o + 64, :]
                if k == 0:
                    dq_ref[rows, cols] = part.astype(BF16)
                else:
                    dqb[k, rows, cols] = part.astype(BF16)
        if k > 0:
            send(dqb.at[k], dqr.at[k], dsend.at[k], drecv.at[k], gdev[k])

    own = None
    for r in order:
        arrival(rr.at[r], rsend.at[r], rrecv.at[r]).wait_recv()
        arrival(rl.at[r], lsend.at[r], lrecv.at[r]).wait_recv()
        t = mine(0, r) + rr[r].astype(F32) + rl[r].astype(F32)
        if r == 0:
            own = t
        else:
            yb[r] = t.astype(BF16)
            send(yb.at[r], yr.at[r], rysend.at[r], ryrecv.at[r], ydev[r])
    for k in range(1, 4):
        arrival(dqr.at[k], dsend.at[k], drecv.at[k]).wait_recv()
    for h in range(2):
        for hd in range(2):
            o = h * UQ + hd * 64
            rows = slice(h * 64, h * 64 + 64)
            cols = slice(hd * HD, hd * HD + HD)
            t = dqa[o : o + 64, :]
            for k in range(1, 4):
                t = t + dqr[k, rows, cols].astype(F32)
            dq_ref[rows, cols] = (t * SCALE).astype(BF16)
    for r in (1, 7, 2, 6, 3, 5, 4):
        arrival(yr.at[r], rysend.at[r], ryrecv.at[r]).wait_recv()
        own = own + yr[r].astype(F32)
    pf[0, :, 0] = own
    for r in range(1, 4):
        o = pl.multiple_of(((zh + r) % 4) * 16, 16)
        zb[r] = pf[0, :, 0, pl.ds(o, 16), :].astype(BF16)
        send(zb.at[r], zr.at[r], zsend.at[r], zrecv.at[r], zdev[r])
    fin = pf[0, :, 0, pl.ds(pl.multiple_of(zh * 16, 16), 16), :]
    for r in range(1, 4):
        arrival(zr.at[r], zsend.at[r], zrecv.at[r]).wait_recv()
        fin = fin + zr[r].astype(F32)
    dk_ref[...] = (fin[0] * SCALE).astype(BF16)
    dv_ref[...] = fin[1].astype(BF16)
    for c in pending:
        c.wait_send()


def local(queries, key_rows, value_rows, out_grad, doc_lengths, span_order):
    vm = pltpu.VMEM
    dma = pltpu.SemaphoreType.DMA
    piece = (2, 64, HD)
    scratch = [
        vm((2, NX, NY, 4, 16, HD), BF16),
        vm((4, 128, 256), BF16),
        vm((4, 128, 256), BF16),
        vm((4, UQ, HD), BF16),
        vm((4, UQ, HD), BF16),
        vm((NX, CK, HD), jnp.int32),
        vm((4, 2, 8, HD), jnp.int32),
        vm((NX, 4, CK, UQ), F32),
        vm((NX, 4, CK, UQ), F32),
        vm((CK, 4 * UQ), BF16),
        vm((CK, 4 * UQ), BF16),
        vm((4 * UQ, HD), F32),
        vm((4, 2, 8, 64, HD), F32),
        vm((3, 4, 2, HD), F32),
        vm((4, 3, 4, 2, HD), F32),
        vm((NX, 4, 5, 8, UQ), F32),
        vm((4, 128, 256), BF16),
        vm((4, 128, 256), BF16),
        vm((4, 8) + piece, BF16),
        vm((8,) + piece, BF16),
        vm((8,) + piece, BF16),
        vm((8,) + piece, BF16),
        vm((8,) + piece, BF16),
        vm((8,) + piece, BF16),
        vm((4, 2, 16, HD), BF16),
        vm((4, 2, 16, HD), BF16),
        dma((4,)),
        dma((4, 2)), dma((4, 2)),
        dma((8,)), dma((8,)),
        dma((8, 3)), dma((8, 3)),
        dma((4,)), dma((4,)),
        dma((4,)), dma((4,)),
        dma((8,)), dma((8,)),
        dma((8,)), dma((8,)),
        dma((8,)), dma((8,)),
        dma((8,)), dma((8,)),
        dma((4,)), dma((4,)),
    ]
    smem = pl.BlockSpec(memory_space=pltpu.SMEM)
    hbm = pl.BlockSpec(memory_space=pl.ANY)
    vmem = pl.BlockSpec(memory_space=pltpu.VMEM)
    return pl.pallas_call(
        kernel,
        out_shape=(
            jax.ShapeDtypeStruct((128, 256), BF16),
            jax.ShapeDtypeStruct((16, HD), BF16),
            jax.ShapeDtypeStruct((16, HD), BF16),
        ),
        in_specs=[smem, smem, hbm, hbm, hbm, hbm],
        out_specs=(vmem, vmem, vmem),
        scratch_shapes=scratch,
        compiler_params=pltpu.CompilerParams(
            collective_id=0, has_side_effects=True, vmem_limit_bytes=60 * 1024 * 1024
        ),
    )(
        doc_lengths,
        span_order,
        queries,
        out_grad,
        key_rows.reshape(4, 2, 16, HD),
        value_rows.reshape(4, 2, 16, HD),
    )


def solution(mesh):
    in_specs = (P("ctx", "head"), P("ctx", None), P("ctx", None), P("ctx", "head"), P(), P())
    out_specs = (P("ctx", "head"), P(("ctx", "head"), None), P(("ctx", "head"), None))
    return jax.shard_map(local, mesh=mesh, in_specs=in_specs, out_specs=out_specs, check_vma=False)
```

```python
import functools
import math

import jax
import jax.numpy as jnp
from jax import lax
from jax.experimental import pallas as pl
from jax.experimental.pallas import tpu as pltpu
from jax.sharding import PartitionSpec as P

MESH = pl.DeviceIdType.MESH
F32 = jnp.float32
BF16 = jnp.bfloat16
NX, NY, NZH = 4, 8, 4
HD = 128
NEG = -1e30
SCALE = HD ** -0.5
EXP_SCALE = SCALE / math.log(2.0)
CK = 512
ROFF = (0, 1, 7, 2, 6, 3, 5, 4)
RPOS = {r: i for i, r in enumerate(ROFF)}
UQ = 256


def swap_rows(v, p):
    parts = [v[(k ^ p) * 2 : (k ^ p) * 2 + 2] for k in range(4)]
    return jnp.concatenate(parts, axis=0)


def kernel(
    lens_ref, order_ref, q_ref, g_ref, k_ref, v_ref,
    dq_ref, dk_ref, dv_ref,
    kv, qa, ga, qs, gs, kp, qlim, es, dps, ws, dss, dqa, pf, stm, st, rst, fac,
    dqb, dqr, sb, m1, rr, rl, yb, yr, zb, zr,
    lsem, qsend, qrecv, ysend, yrecv, xsend, xrecv, ssend, srecv, dsend, drecv,
    m1send, m1recv, rsend, rrecv, lsend, lrecv, rysend, ryrecv, zsend, zrecv,
    upsem, dnsem, nearsem,
):
    ctx = lax.axis_index("ctx")
    head = lax.axis_index("head")
    zl, y, x = ctx // 32, (ctx // 4) % 8, ctx % 4
    zh, core = head // 2, head % 2

    def at(zl_, y_, x_):
        return zl_ * 32 + y_ * 4 + x_

    right = (at(zl, y, (x + 1) % 4), head)
    left = (at(zl, y, (x + 3) % 4), head)
    ydev = [(at(zl, (y + r) % 8, x), head) for r in range(8)]
    zdev = [(ctx, ((zh + r) % 4) * 2 + core) for r in range(4)]
    gdev = [
        (at((zl + k // 2) % 2, y, x), zh * 2 + (core + k % 2) % 2) for k in range(4)
    ]
    zout = (at(1 - zl, y, x), ((zh + 3 + 2 * zl) % 4) * 2 + core)

    stage = [
        pltpu.make_async_copy(k_ref.at[:, core], kv.at[0, 0, 0], lsem.at[0]),
        pltpu.make_async_copy(v_ref.at[:, core], kv.at[1, 0, 0], lsem.at[1]),
        pltpu.make_async_copy(q_ref, qa.at[0], lsem.at[2]),
        pltpu.make_async_copy(g_ref, ga.at[0], lsem.at[3]),
    ]
    for c in stage:
        c.start()

    def signal(sem, dev):
        pl.semaphore_signal(sem, inc=1, device_id=dev, device_id_type=MESH)

    barrier = pltpu.get_barrier_semaphore()
    peers = [right, left, ydev[1], ydev[7], zout] + gdev[1:]
    for p in peers:
        signal(barrier, p)
    pl.semaphore_wait(barrier, len(peers))

    pending = []

    def send(src, dst, ss, rs, dev):
        c = pltpu.make_async_remote_copy(
            src_ref=src, dst_ref=dst, send_sem=ss, recv_sem=rs,
            device_id=dev, device_id_type=MESH,
        )
        c.start()
        pending.append(c)

    def landed(dst, ss, rs):
        pltpu.make_async_remote_copy(
            src_ref=dst, dst_ref=dst, send_sem=ss, recv_sem=rs,
            device_id=right, device_id_type=MESH,
        ).wait_recv()

    def blk(xr, r):
        return kv.at[:, RPOS[r % 8], xr]

    def x_forward(r):
        r = r % 8
        send(blk(0, r), blk(3, r), xsend.at[r, 0], xrecv.at[r, 0], right)
        send(blk(0, r), blk(1, r), xsend.at[r, 1], xrecv.at[r, 1], left)

    def y_send(r):
        r = r % 8
        send(blk(0, 0), blk(0, -r), ysend.at[r], yrecv.at[r], ydev[r])

    def y_landed(r):
        i = (-r) % 8
        landed(blk(0, r), ysend.at[i], yrecv.at[i])

    def x_arrive(r):
        r = r % 8
        landed(blk(3, r), xsend.at[r, 0], xrecv.at[r, 0])
        if r % 2 == 0:
            send(blk(3, r), blk(2, r), xsend.at[r, 2], xrecv.at[r, 2], right)
        landed(blk(1, r), xsend.at[r, 1], xrecv.at[r, 1])
        if r % 2 == 1:
            send(blk(1, r), blk(2, r), xsend.at[r, 2], xrecv.at[r, 2], left)

    def x_last(r):
        r = r % 8
        landed(blk(2, r), xsend.at[r, 2], xrecv.at[r, 2])

    signal(nearsem.at[0], zout)
    signal(nearsem.at[1], gdev[2])
    signal(upsem.at[0], ydev[1])
    signal(dnsem.at[0], ydev[7])
    stage[0].wait()
    stage[1].wait()
    y_send(1)
    y_send(7)
    x_forward(0)
    for k in (1, 2):
        send(q_ref, qa.at[k], qsend.at[k, 0], qrecv.at[k, 0], gdev[k])
        send(g_ref, ga.at[k], qsend.at[k, 1], qrecv.at[k, 1], gdev[k])
    pl.semaphore_wait(upsem.at[0], 1)
    signal(upsem.at[1], ydev[1])
    y_send(6)
    pl.semaphore_wait(dnsem.at[0], 1)
    signal(dnsem.at[1], ydev[7])
    y_send(2)
    pl.semaphore_wait(nearsem.at[0], 1)
    pl.semaphore_wait(nearsem.at[1], 1)
    signal(nearsem.at[2], zdev[3])
    pl.semaphore_wait(upsem.at[1], 1)
    signal(upsem.at[2], ydev[1])
    y_send(5)
    pl.semaphore_wait(dnsem.at[1], 1)
    y_send(3)
    pl.semaphore_wait(upsem.at[2], 1)
    y_send(4)

    lane = lax.broadcasted_iota(jnp.int32, (8, HD), 1) % 64
    starts = []
    total = jnp.int32(0)
    for i in range(8):
        starts.append(total)
        total = total + lens_ref[i]
    for dz in range(2):
        octx = at((zl + dz) % 2, y, x)
        for h in range(2):
            u = dz * 2 + h
            qp = order_ref[h, octx] * 64 + lane
            first = jnp.zeros_like(qp)
            for s in starts:
                first = jnp.maximum(first, jnp.where(qp >= s, s, 0))
            qlim[u, 0] = qp
            qlim[u, 1] = first
    row = lax.broadcasted_iota(jnp.int32, (32, HD), 0)
    pattern = (row // 16) * 32 + row % 16 + core * 16
    for rp in range(8):
        for xr in range(4):
            octx = at(zl, (y + ROFF[rp]) % 8, (x + xr) % 4)
            for h in range(2):
                o = ((rp % 2) * 4 + xr) * 64 + h * 32
                kp[rp // 2, o : o + 32, :] = pattern + order_ref[h, octx] * 64

    def units(dz):
        for h in range(2):
            u = dz * 2 + h
            for dc in range(2):
                for hd in range(2):
                    rows = slice(h * 64, h * 64 + 64)
                    cols = slice(hd * HD, hd * HD + HD)
                    o = (dc * 2 + hd) * 64
                    qs[u, o : o + 64, :] = qa[dz * 2 + dc, rows, cols]
                    gs[u, o : o + 64, :] = ga[dz * 2 + dc, rows, cols]

    def pass1(j, dz):
        keys = kv[0, 2 * j : 2 * j + 2].reshape(CK, HD)
        vals = kv[1, 2 * j : 2 * j + 2].reshape(CK, HD)
        dims = (((1,), (1,)), ((), ()))
        for h in range(2):
            u = dz * 2 + h
            s = lax.dot_general(keys, qs[u], dims, preferred_element_type=F32)
            dp = lax.dot_general(vals, gs[u], dims, preferred_element_type=F32)
            dps[j, u] = dp
            pos = kp[j]
            allowed = (pos <= qlim[u, 0, 0:1, :]) & (pos >= qlim[u, 1, 0:1, :])
            for dc in range(2):
                cols = slice(dc * HD, dc * HD + HD)
                row = (dz * 2 + dc) * 2 + h
                sh = jnp.where(allowed, s[:, cols], NEG)
                m = jnp.max(sh, axis=0, keepdims=True)
                e = jnp.exp2((sh - m) * EXP_SCALE)
                es[j, u, :, cols] = e
                stm[j, 0, row : row + 1, :] = m
                stm[j, 1, row : row + 1, :] = jnp.sum(e, axis=0, keepdims=True)
                stm[j, 2, row : row + 1, :] = jnp.sum(e * dp[:, cols], axis=0, keepdims=True)

    def q_landed(k):
        landed(qa.at[k], qsend.at[k, 0], qrecv.at[k, 0])
        landed(ga.at[k], qsend.at[k, 1], qrecv.at[k, 1])

    y_landed(1)
    x_forward(1)
    y_landed(7)
    x_forward(7)
    x_arrive(0)
    stage[2].wait()
    stage[3].wait()
    q_landed(1)
    units(0)
    y_landed(2)
    x_forward(2)
    y_landed(6)
    x_forward(6)
    q_landed(2)
    send(qa.at[2], qa.at[3], qsend.at[3, 0], qrecv.at[3, 0], gdev[1])
    send(ga.at[2], ga.at[3], qsend.at[3, 1], qrecv.at[3, 1], gdev[1])
    x_arrive(1)
    x_arrive(7)
    y_landed(3)
    x_forward(3)
    y_landed(5)
    x_forward(5)
    x_last(0)
    x_last(1)
    pass1(0, 0)
    y_landed(4)
    x_forward(4)
    x_arrive(2)
    x_arrive(6)
    q_landed(3)
    units(1)
    pass1(0, 1)
    x_arrive(3)
    x_arrive(5)
    x_last(7)
    x_last(2)
    pass1(1, 0)
    x_arrive(4)
    pass1(1, 1)
    x_last(6)
    x_last(3)
    pass1(2, 0)
    pass1(2, 1)
    x_last(5)
    x_last(4)
    pass1(3, 0)
    pass1(3, 1)
    pl.semaphore_wait(nearsem.at[2], 1)

    def top(vals):
        return jnp.maximum(jnp.maximum(vals[0], vals[1]), jnp.maximum(vals[2], vals[3]))

    ms = [stm[j, 0] for j in range(4)]
    m = top(ms)
    sc = [jnp.exp2((a - m) * EXP_SCALE) for a in ms]
    st[0] = m
    st[1] = sum(sc[j] * stm[j, 1] for j in range(4))
    st[2] = sum(sc[j] * stm[j, 2] for j in range(4))
    for k in range(1, 4):
        send(st, rst.at[k], ssend.at[k], srecv.at[k], gdev[k])
    for k in range(1, 4):
        landed(rst.at[k], ssend.at[k], srecv.at[k])
    got = [[st[i]] + [swap_rows(rst[p, i], p) for p in range(1, 4)] for i in range(3)]
    gm = top(got[0])
    sc = [jnp.exp2((a - gm) * EXP_SCALE) for a in got[0]]
    inv = 1.0 / sum(sc[p] * got[1][p] for p in range(4))
    fac[4] = sum(sc[p] * got[2][p] for p in range(4)) * inv
    for j in range(4):
        fac[j] = jnp.exp2((ms[j] - gm) * EXP_SCALE) * inv

    def column(c, first):
        for u in range(4):
            dz, h = u // 2, u % 2
            for dc in range(2):
                row = (dz * 2 + dc) * 2 + h
                cols = slice(dc * HD, dc * HD + HD)
                o = u * UQ + dc * HD
                delta = fac[4, row : row + 1, :]
                for rp in range(8):
                    j = rp // 2
                    ko = ((rp % 2) * 4 + c) * 64
                    w = es[j, u, ko : ko + 64, cols] * fac[j, row : row + 1, :]
                    ws[rp * 64 : rp * 64 + 64, o : o + HD] = w.astype(BF16)
                    d = w * (dps[j, u, ko : ko + 64, cols] - delta)
                    dss[rp * 64 : rp * 64 + 64, o : o + HD] = d.astype(BF16)
        dims = (((1,), (0,)), ((), ()))
        q_all = qs[...].reshape(4 * UQ, HD)
        g_all = gs[...].reshape(4 * UQ, HD)
        dkc = lax.dot_general(dss[...], q_all, dims, preferred_element_type=F32)
        pf[c, 0] = dkc.reshape(8, 64, HD)
        dvc = lax.dot_general(ws[...], g_all, dims, preferred_element_type=F32)
        pf[c, 1] = dvc.reshape(8, 64, HD)
        keys = kv[0, :, c].reshape(CK, HD)
        part = lax.dot_general(
            dss[...], keys, (((0,), (0,)), ((), ())), preferred_element_type=F32
        )
        if first:
            dqa[...] = part
        else:
            dqa[...] += part

    def mine(c, r):
        return pf[c, :, RPOS[r]]

    order = [4, 3, 5, 2, 6, 1, 7, 0]
    column(2, True)
    for r in order:
        sb[2, r] = mine(2, r).astype(BF16)
        dev = right if r % 2 == 0 else left
        send(sb.at[2, r], m1.at[r], m1send.at[r], m1recv.at[r], dev)
    column(1, False)
    for r in order:
        if r % 2 == 1:
            sb[1, r] = mine(1, r).astype(BF16)
            send(sb.at[1, r], rr.at[r], rsend.at[r], rrecv.at[r], right)
    column(3, False)
    for r in order:
        if r % 2 == 0:
            sb[3, r] = mine(3, r).astype(BF16)
            send(sb.at[3, r], rl.at[r], lsend.at[r], lrecv.at[r], left)
    for r in order:
        landed(m1.at[r], m1send.at[r], m1recv.at[r])
        c = 1 if r % 2 == 0 else 3
        sb[c, r] = (mine(c, r) + m1[r].astype(F32)).astype(BF16)
        if r % 2 == 0:
            send(sb.at[1, r], rr.at[r], rsend.at[r], rrecv.at[r], right)
        else:
            send(sb.at[3, r], rl.at[r], lsend.at[r], lrecv.at[r], left)
    column(0, False)

    for k in range(4):
        dz, dc = k // 2, k % 2
        for h in range(2):
            for hd in range(2):
                o = (dz * 2 + h) * UQ + (dc * 2 + hd) * 64
                rows = slice(h * 64, h * 64 + 64)
                cols = slice(hd * HD, hd * HD + HD)
                part = dqa[o : o + 64, :]
                if k == 0:
                    dq_ref[rows, cols] = part.astype(BF16)
                else:
                    dqb[k, rows, cols] = part.astype(BF16)
        if k > 0:
            send(dqb.at[k], dqr.at[k], dsend.at[k], drecv.at[k], gdev[k])

    own = None
    for r in order:
        landed(rr.at[r], rsend.at[r], rrecv.at[r])
        landed(rl.at[r], lsend.at[r], lrecv.at[r])
        t = mine(0, r) + rr[r].astype(F32) + rl[r].astype(F32)
        if r == 0:
            own = t
        else:
            yb[r] = t.astype(BF16)
            send(yb.at[r], yr.at[r], rysend.at[r], ryrecv.at[r], ydev[r])
    for k in range(1, 4):
        landed(dqr.at[k], dsend.at[k], drecv.at[k])
    for h in range(2):
        for hd in range(2):
            o = h * UQ + hd * 64
            rows = slice(h * 64, h * 64 + 64)
            cols = slice(hd * HD, hd * HD + HD)
            t = dqa[o : o + 64, :]
            for k in range(1, 4):
                t = t + dqr[k, rows, cols].astype(F32)
            dq_ref[rows, cols] = (t * SCALE).astype(BF16)
    for r in (1, 7, 2, 6, 3, 5, 4):
        landed(yr.at[r], rysend.at[r], ryrecv.at[r])
        own = own + yr[r].astype(F32)
    pf[0, :, 0] = own
    for r in range(1, 4):
        o = pl.multiple_of(((zh + r) % 4) * 16, 16)
        zb[r] = pf[0, :, 0, pl.ds(o, 16), :].astype(BF16)
        send(zb.at[r], zr.at[r], zsend.at[r], zrecv.at[r], zdev[r])
    fin = pf[0, :, 0, pl.ds(pl.multiple_of(zh * 16, 16), 16), :]
    for r in range(1, 4):
        landed(zr.at[r], zsend.at[r], zrecv.at[r])
        fin = fin + zr[r].astype(F32)
    dk_ref[...] = (fin[0] * SCALE).astype(BF16)
    dv_ref[...] = fin[1].astype(BF16)
    for c in pending:
        c.wait_send()


def local(queries, key_rows, value_rows, out_grad, doc_lengths, span_order):
    vm = pltpu.VMEM
    dma = pltpu.SemaphoreType.DMA
    piece = (2, 64, HD)
    scratch = [
        vm((2, NY, NX, 4, 16, HD), BF16),
        vm((4, 128, 256), BF16),
        vm((4, 128, 256), BF16),
        vm((4, UQ, HD), BF16),
        vm((4, UQ, HD), BF16),
        vm((NX, CK, HD), jnp.int32),
        vm((4, 2, 8, HD), jnp.int32),
        vm((NX, 4, CK, UQ), F32),
        vm((NX, 4, CK, UQ), F32),
        vm((CK, 4 * UQ), BF16),
        vm((CK, 4 * UQ), BF16),
        vm((4 * UQ, HD), F32),
        vm((4, 2, 8, 64, HD), F32),
        vm((4, 3, 8, HD), F32),
        vm((3, 8, HD), F32),
        vm((4, 3, 8, HD), F32),
        vm((5, 8, HD), F32),
        vm((4, 128, 256), BF16),
        vm((4, 128, 256), BF16),
        vm((4, 8) + piece, BF16),
        vm((8,) + piece, BF16),
        vm((8,) + piece, BF16),
        vm((8,) + piece, BF16),
        vm((8,) + piece, BF16),
        vm((8,) + piece, BF16),
        vm((4, 2, 16, HD), BF16),
        vm((4, 2, 16, HD), BF16),
        dma((4,)),
        dma((4, 2)), dma((4, 2)),
        dma((8,)), dma((8,)),
        dma((8, 3)), dma((8, 3)),
        dma((4,)), dma((4,)),
        dma((4,)), dma((4,)),
        dma((8,)), dma((8,)),
        dma((8,)), dma((8,)),
        dma((8,)), dma((8,)),
        dma((8,)), dma((8,)),
        dma((4,)), dma((4,)),
        pltpu.SemaphoreType.REGULAR((3,)),
        pltpu.SemaphoreType.REGULAR((2,)),
        pltpu.SemaphoreType.REGULAR((3,)),
    ]
    smem = pl.BlockSpec(memory_space=pltpu.SMEM)
    hbm = pl.BlockSpec(memory_space=pl.ANY)
    vmem = pl.BlockSpec(memory_space=pltpu.VMEM)
    return pl.pallas_call(
        kernel,
        out_shape=(
            vm((128, 256), BF16),
            vm((16, HD), BF16),
            vm((16, HD), BF16),
        ),
        in_specs=[smem, smem, hbm, hbm, hbm, hbm],
        out_specs=(vmem, vmem, vmem),
        scratch_shapes=scratch,
        compiler_params=pltpu.CompilerParams(
            collective_id=0, has_side_effects=True, vmem_limit_bytes=60 * 1024 * 1024
        ),
    )(
        doc_lengths,
        span_order.T,
        queries,
        out_grad,
        key_rows.reshape(4, 2, 16, HD),
        value_rows.reshape(4, 2, 16, HD),
    )


def solution(mesh):
    in_specs = (P("ctx", "head"), P("ctx", None), P("ctx", None), P("ctx", "head"), P(), P())
    out_specs = (P("ctx", "head"), P(("ctx", "head"), None), P(("ctx", "head"), None))
    return jax.shard_map(local, mesh=mesh, in_specs=in_specs, out_specs=out_specs, check_vma=False)
```

```python
import functools
import math

import jax
import jax.numpy as jnp
from jax import lax
from jax.experimental import pallas as pl
from jax.experimental.pallas import tpu as pltpu
from jax.sharding import PartitionSpec as P

MESH = pl.DeviceIdType.MESH
F32 = jnp.float32
BF16 = jnp.bfloat16
NU = 8
HD = 128
NEG = -1e30
SCALE = HD ** -0.5
EXP_SCALE = SCALE / math.log(2.0)
CK = 256
ROFF = (0, 1, 7, 2, 6, 3, 5, 4)
RPOS = {r: i for i, r in enumerate(ROFF)}
UQ = 256


def swap_rows(v, p):
    parts = [v[(k ^ p) * 2 : (k ^ p) * 2 + 2] for k in range(4)]
    return jnp.concatenate(parts, axis=0)


def kernel(
    lens_ref, order_ref, q_ref, g_ref, k_ref, v_ref,
    dq_ref, dk_ref, dv_ref,
    kv, qa, ga, qs, gs, kp, qlim, es, dps, ws, dss, dqa, pf, stm, st, rst, fac,
    dqb, dqr, sb, xr, yb, yr, zb, zr,
    lsem, qsend, qrecv, ysend, yrecv, xsend, xrecv, ssend, srecv, dsend, drecv,
    rsend, rrecv, rysend, ryrecv, zsend, zrecv, nearsem,
):
    ctx = lax.axis_index("ctx")
    head = lax.axis_index("head")
    zl, y, x = ctx // 32, (ctx // 4) % 8, ctx % 4
    zh, core = head // 2, head % 2
    xg = x + 1 - 2 * (x % 2)
    xo = (x + 3 + 2 * (x % 2)) % 4

    def at(zl_, y_, x_):
        return zl_ * 32 + y_ * 4 + x_

    odev = (at(zl, y, xo), head)
    ydev = [(at(zl, (y + r) % 8, x), head) for r in range(8)]
    zdev = [(ctx, ((zh + r) % 4) * 2 + core) for r in range(4)]
    gdev = [
        (
            at((zl + (k // 2) % 2) % 2, y, xg if k // 4 else x),
            zh * 2 + (core + k % 2) % 2,
        )
        for k in range(8)
    ]
    zout = (at(1 - zl, y, x), ((zh + 3 + 2 * zl) % 4) * 2 + core)

    stage = [
        pltpu.make_async_copy(k_ref.at[:, core], kv.at[0, 0, 0], lsem.at[0]),
        pltpu.make_async_copy(v_ref.at[:, core], kv.at[1, 0, 0], lsem.at[1]),
        pltpu.make_async_copy(q_ref, qa.at[0], lsem.at[2]),
        pltpu.make_async_copy(g_ref, ga.at[0], lsem.at[3]),
    ]
    for c in stage:
        c.start()

    def signal(sem, dev):
        pl.semaphore_signal(sem, inc=1, device_id=dev, device_id_type=MESH)

    barrier = pltpu.get_barrier_semaphore()
    peers = [odev, ydev[1], ydev[7], ydev[2], ydev[6], zout] + gdev[1:]
    for p in peers:
        signal(barrier, p)
    pl.semaphore_wait(barrier, len(peers))

    pending = []

    def send(src, dst, ss, rs, dev):
        c = pltpu.make_async_remote_copy(
            src_ref=src, dst_ref=dst, send_sem=ss, recv_sem=rs,
            device_id=dev, device_id_type=MESH,
        )
        c.start()
        pending.append(c)

    def landed(dst, ss, rs):
        pltpu.make_async_remote_copy(
            src_ref=dst, dst_ref=dst, send_sem=ss, recv_sem=rs,
            device_id=odev, device_id_type=MESH,
        ).wait_recv()

    def blk(i, c, r):
        return kv.at[i, RPOS[r % 8], c]

    def x_forward(r):
        r = r % 8
        for i in range(2):
            send(blk(i, 0, r), blk(i, 1, r), xsend.at[r, i], xrecv.at[r, i], odev)

    def x_landed(r):
        r = r % 8
        for i in range(2):
            landed(blk(i, 1, r), xsend.at[r, i], xrecv.at[r, i])

    def y_send(i, src, dst, to, sem):
        send(blk(i, 0, src), blk(i, 0, dst), ysend.at[sem, i], yrecv.at[sem, i], ydev[to])

    def y_landed(i, r, sem):
        landed(blk(i, 0, r), ysend.at[sem, i], yrecv.at[sem, i])

    stage[0].wait()
    y_send(0, 0, 6, 2, 2)
    y_send(0, 0, 2, 6, 6)
    stage[1].wait()
    y_send(1, 0, 6, 2, 2)
    y_send(1, 0, 2, 6, 6)
    x_forward(0)
    for i in range(2):
        y_send(i, 0, 7, 1, 1)
        y_send(i, 0, 1, 7, 7)
    for k in (2, 4, 1):
        send(q_ref, qa.at[k], qsend.at[k, 0], qrecv.at[k, 0], gdev[k])
        send(g_ref, ga.at[k], qsend.at[k, 1], qrecv.at[k, 1], gdev[k])
    signal(nearsem.at[0], zout)
    signal(nearsem.at[1], gdev[2])

    lane = lax.broadcasted_iota(jnp.int32, (8, HD), 1) % 64
    starts = []
    total = jnp.int32(0)
    for i in range(8):
        starts.append(total)
        total = total + lens_ref[i]
    for g in range(4):
        octx = at((zl + g % 2) % 2, y, xg if g // 2 else x)
        for h in range(2):
            u = g * 2 + h
            qp = order_ref[h, octx] * 64 + lane
            first = jnp.zeros_like(qp)
            for s in starts:
                first = jnp.maximum(first, jnp.where(qp >= s, s, 0))
            qlim[u, 0] = qp
            qlim[u, 1] = first
    row = lax.broadcasted_iota(jnp.int32, (32, HD), 0)
    pattern = (row // 16) * 32 + row % 16 + core * 16
    for rp in range(8):
        for c in range(2):
            octx = at(zl, (y + ROFF[rp]) % 8, xo if c else x)
            for h in range(2):
                o = ((rp % 2) * 2 + c) * 64 + h * 32
                kp[rp // 2, o : o + 32, :] = pattern + order_ref[h, octx] * 64

    def units(g):
        for h in range(2):
            u = g * 2 + h
            for dc in range(2):
                for hd in range(2):
                    rows = slice(h * 64, h * 64 + 64)
                    cols = slice(hd * HD, hd * HD + HD)
                    o = (dc * 2 + hd) * 64
                    qs[u, o : o + 64, :] = qa[g * 2 + dc, rows, cols]
                    gs[u, o : o + 64, :] = ga[g * 2 + dc, rows, cols]

    def pass1(j, g):
        keys = kv[0, 2 * j : 2 * j + 2].reshape(CK, HD)
        vals = kv[1, 2 * j : 2 * j + 2].reshape(CK, HD)
        dims = (((1,), (1,)), ((), ()))
        for h in range(2):
            u = g * 2 + h
            s = lax.dot_general(keys, qs[u], dims, preferred_element_type=F32)
            dp = lax.dot_general(vals, gs[u], dims, preferred_element_type=F32)
            dps[j, u] = dp
            pos = kp[j]
            allowed = (pos <= qlim[u, 0, 0:1, :]) & (pos >= qlim[u, 1, 0:1, :])
            for dc in range(2):
                cols = slice(dc * HD, dc * HD + HD)
                row = (g * 2 + dc) * 2 + h
                sh = jnp.where(allowed, s[:, cols], NEG)
                m = jnp.max(sh, axis=0, keepdims=True)
                e = jnp.exp2((sh - m) * EXP_SCALE)
                es[j, u, :, cols] = e
                stm[j, 0, row : row + 1, :] = m
                stm[j, 1, row : row + 1, :] = jnp.sum(e, axis=0, keepdims=True)
                stm[j, 2, row : row + 1, :] = jnp.sum(e * dp[:, cols], axis=0, keepdims=True)

    def q_landed(k):
        landed(qa.at[k], qsend.at[k, 0], qrecv.at[k, 0])

    def g_landed(k):
        landed(ga.at[k], qsend.at[k, 1], qrecv.at[k, 1])

    def q_pass(k, to, dev):
        send(qa.at[k], qa.at[to], qsend.at[to, 0], qrecv.at[to, 0], dev)

    def g_pass(k, to, dev):
        send(ga.at[k], ga.at[to], qsend.at[to, 1], qrecv.at[to, 1], dev)

    stage[2].wait()
    stage[3].wait()
    q_landed(1)
    g_landed(1)
    units(0)
    for i in range(2):
        y_landed(i, 6, 2)
        y_send(i, 6, 5, 1, 3)
        if i == 0:
            y_send(0, 6, 4, 2, 4)
        y_landed(i, 2, 6)
        y_send(i, 2, 3, 7, 5)
        if i == 1:
            y_send(1, 2, 4, 6, 4)
    for i in range(2):
        y_landed(i, 7, 1)
        y_landed(i, 1, 7)
    x_forward(7)
    x_forward(1)
    x_forward(2)
    x_forward(6)
    q_landed(2)
    q_pass(2, 6, gdev[4])
    q_pass(2, 3, gdev[1])
    q_landed(4)
    q_pass(4, 5, gdev[1])
    g_landed(4)
    g_pass(4, 6, gdev[2])
    g_pass(4, 5, gdev[1])
    g_landed(2)
    g_pass(2, 3, gdev[1])
    x_landed(0)
    x_landed(1)
    pl.semaphore_wait(nearsem.at[0], 1)
    pl.semaphore_wait(nearsem.at[1], 1)
    signal(nearsem.at[2], zdev[3])
    pass1(0, 0)
    for i in range(2):
        y_landed(i, 5, 3)
    x_forward(5)
    for i in range(2):
        y_landed(i, 3, 5)
    x_forward(3)
    y_landed(0, 4, 4)
    y_landed(1, 4, 4)
    x_forward(4)
    q_landed(6)
    q_pass(6, 7, gdev[1])
    g_landed(6)
    g_pass(6, 7, gdev[1])
    q_landed(3)
    g_landed(3)
    units(1)
    pass1(0, 1)
    q_landed(5)
    g_landed(5)
    units(2)
    pass1(0, 2)
    x_landed(7)
    x_landed(2)
    pass1(1, 0)
    pass1(1, 1)
    pass1(1, 2)
    q_landed(7)
    g_landed(7)
    units(3)
    pass1(0, 3)
    pass1(1, 3)
    x_landed(6)
    x_landed(3)
    for g in range(4):
        pass1(2, g)
    x_landed(5)
    x_landed(4)
    def top(vals):
        while len(vals) > 1:
            vals = [jnp.maximum(a, b) for a, b in zip(vals[::2], vals[1::2])]
        return vals[0]

    def own_stats(dx):
        rows = slice(dx * 8, dx * 8 + 8)
        ms = [stm[j, 0, rows] for j in range(4)]
        m = top(ms)
        sc = [jnp.exp2((a - m) * EXP_SCALE) for a in ms]
        st[dx, 0] = m
        st[dx, 1] = sum(sc[j] * stm[j, 1, rows] for j in range(4))
        st[dx, 2] = sum(sc[j] * stm[j, 2, rows] for j in range(4))
        for k in (6, 7, 4, 5, 2, 3, 1):
            to = rst.at[k, (dx + k // 4) % 2]
            send(st.at[dx], to, ssend.at[k, dx], srecv.at[k, (dx + k // 4) % 2], gdev[k])

    pass1(3, 0)
    pass1(3, 1)
    own_stats(0)
    pass1(3, 2)
    pass1(3, 3)
    own_stats(1)
    pl.semaphore_wait(nearsem.at[2], 1)
    for dx in range(2):
        rows = slice(dx * 8, dx * 8 + 8)
        for k in range(1, 8):
            landed(rst.at[k, dx], ssend.at[k, dx], srecv.at[k, dx])
        got = [[st[dx, i]] + [swap_rows(rst[p, dx, i], p % 4) for p in range(1, 8)] for i in range(3)]
        gm = top(got[0])
        sc = [jnp.exp2((a - gm) * EXP_SCALE) for a in got[0]]
        inv = 1.0 / sum(sc[p] * got[1][p] for p in range(8))
        fac[4, rows] = sum(sc[p] * got[2][p] for p in range(8)) * inv
        for j in range(4):
            fac[j, rows] = jnp.exp2((stm[j, 0, rows] - gm) * EXP_SCALE) * inv

    def block(c, j0, nj, first):
        nk = nj * 128
        for u in range(NU):
            g, h = u // 2, u % 2
            for dc in range(2):
                row = (g * 2 + dc) * 2 + h
                cols = slice(dc * HD, dc * HD + HD)
                o = u * UQ + dc * HD
                delta = fac[4, row : row + 1, :]
                for i in range(2 * nj):
                    j = j0 + i // 2
                    ko = ((i % 2) * 2 + c) * 64
                    w = es[j, u, ko : ko + 64, cols] * fac[j, row : row + 1, :]
                    ws[i * 64 : i * 64 + 64, o : o + HD] = w.astype(BF16)
                    d = w * (dps[j, u, ko : ko + 64, cols] - delta)
                    dss[i * 64 : i * 64 + 64, o : o + HD] = d.astype(BF16)
        dims = (((1,), (0,)), ((), ()))
        q_all = qs[...].reshape(NU * UQ, HD)
        g_all = gs[...].reshape(NU * UQ, HD)
        r0, n = 2 * j0, 2 * nj
        dkc = lax.dot_general(dss[0:nk], q_all, dims, preferred_element_type=F32)
        pf[c, 0, r0 : r0 + n] = dkc.reshape(n, 64, HD)
        dvc = lax.dot_general(ws[0:nk], g_all, dims, preferred_element_type=F32)
        pf[c, 1, r0 : r0 + n] = dvc.reshape(n, 64, HD)
        keys = kv[0, r0 : r0 + n, c].reshape(nk, HD)
        add = lax.dot_general(
            dss[0:nk], keys, (((0,), (0,)), ((), ())), preferred_element_type=F32
        )
        if first:
            dqa[...] = add
        else:
            dqa[...] += add

    def mine(c, r):
        return pf[c, :, RPOS[r]]

    def x_send(r):
        sb[r] = mine(1, r).astype(BF16)
        send(sb.at[r], xr.at[r], rsend.at[r], rrecv.at[r], odev)

    def column_sum(r):
        landed(xr.at[r], rsend.at[r], rrecv.at[r])
        return mine(0, r) + xr[r].astype(F32)

    def y_out(r, to):
        send(yb.at[r], yr.at[r], rysend.at[r], ryrecv.at[r], ydev[to])

    def y_in(r):
        landed(yr.at[r], rysend.at[r], ryrecv.at[r])

    block(1, 3, 1, True)
    x_send(4)
    x_send(5)
    block(1, 2, 1, False)
    x_send(3)
    x_send(6)
    block(0, 2, 2, False)
    block(1, 0, 2, False)
    for r in (2, 1, 7, 0):
        x_send(r)
    yb[4] = column_sum(4).astype(BF16)
    send(yb.at[4, 0], yr.at[4, 0], rysend.at[4], ryrecv.at[4], ydev[2])
    send(yb.at[4, 1], yr.at[4, 1], rysend.at[0], ryrecv.at[0], ydev[6])
    block(0, 0, 2, False)
    yb[5] = column_sum(5).astype(BF16)
    y_out(5, 7)
    yb[3] = column_sum(3).astype(BF16)
    y_out(3, 1)

    def dq_part(k, h, hd):
        o = ((k // 2) * 2 + h) * UQ + ((k % 2) * 2 + hd) * 64
        return dqa[o : o + 64, :]

    for k in (6, 7, 4, 5, 2, 3, 1):
        for h in range(2):
            for hd in range(2):
                rows = slice(h * 64, h * 64 + 64)
                cols = slice(hd * HD, hd * HD + HD)
                dqb[k, rows, cols] = dq_part(k, h, hd).astype(BF16)
        send(dqb.at[k], dqr.at[k], dsend.at[k], drecv.at[k], gdev[k])

    t6 = column_sum(6)
    t2 = column_sum(2)
    y_in(5)
    landed(yr.at[4, 1], rysend.at[0], ryrecv.at[0])
    yb[6, 0] = (t6[0] + yr[5, 0].astype(F32)).astype(BF16)
    yb[6, 1] = (t6[1] + yr[5, 1].astype(F32) + yr[4, 1].astype(F32)).astype(BF16)
    y_out(6, 6)
    y_in(3)
    landed(yr.at[4, 0], rysend.at[4], ryrecv.at[4])
    yb[2, 0] = (t2[0] + yr[3, 0].astype(F32) + yr[4, 0].astype(F32)).astype(BF16)
    yb[2, 1] = (t2[1] + yr[3, 1].astype(F32)).astype(BF16)
    y_out(2, 2)
    yb[1] = column_sum(1).astype(BF16)
    y_out(1, 1)
    yb[7] = column_sum(7).astype(BF16)
    y_out(7, 7)
    own = column_sum(0)
    for r in (1, 7, 2, 6):
        y_in(r)
        own = own + yr[r].astype(F32)
    pf[0, :, 0] = own
    for r in (2, 1, 3):
        o = pl.multiple_of(((zh + r) % 4) * 16, 16)
        zb[r] = pf[0, :, 0, pl.ds(o, 16), :].astype(BF16)
        send(zb.at[r], zr.at[r], zsend.at[r], zrecv.at[r], zdev[r])
    fin = pf[0, :, 0, pl.ds(pl.multiple_of(zh * 16, 16), 16), :]
    for k in range(1, 8):
        landed(dqr.at[k], dsend.at[k], drecv.at[k])
    for h in range(2):
        for hd in range(2):
            rows = slice(h * 64, h * 64 + 64)
            cols = slice(hd * HD, hd * HD + HD)
            t = dq_part(0, h, hd)
            for k in range(1, 8):
                t = t + dqr[k, rows, cols].astype(F32)
            dq_ref[rows, cols] = (t * SCALE).astype(BF16)
    for c in pending:
        c.wait_send()
    for r in (1, 3, 2):
        landed(zr.at[r], zsend.at[r], zrecv.at[r])
        fin = fin + zr[r].astype(F32)
    dk_ref[...] = (fin[0] * SCALE).astype(BF16)
    dv_ref[...] = fin[1].astype(BF16)


def local(queries, key_rows, value_rows, out_grad, doc_lengths, span_order):
    vm = pltpu.VMEM
    dma = pltpu.SemaphoreType.DMA
    piece = (2, 64, HD)
    scratch = [
        vm((2, 8, 2, 4, 16, HD), BF16),
        vm((8, 128, 256), BF16),
        vm((8, 128, 256), BF16),
        vm((NU, UQ, HD), BF16),
        vm((NU, UQ, HD), BF16),
        vm((4, CK, HD), jnp.int32),
        vm((NU, 2, 8, HD), jnp.int32),
        vm((4, NU, CK, UQ), F32),
        vm((4, NU, CK, UQ), F32),
        vm((CK, NU * UQ), BF16),
        vm((CK, NU * UQ), BF16),
        vm((NU * UQ, HD), F32),
        vm((2, 2, 8, 64, HD), F32),
        vm((4, 3, 16, HD), F32),
        vm((2, 3, 8, HD), F32),
        vm((8, 2, 3, 8, HD), F32),
        vm((5, 16, HD), F32),
        vm((8, 128, 256), BF16),
        vm((8, 128, 256), BF16),
        vm((8,) + piece, BF16),
        vm((8,) + piece, BF16),
        vm((8,) + piece, BF16),
        vm((8,) + piece, BF16),
        vm((4, 2, 16, HD), BF16),
        vm((4, 2, 16, HD), BF16),
        dma((4,)),
        dma((8, 2)), dma((8, 2)),
        dma((8, 2)), dma((8, 2)),
        dma((8, 2)), dma((8, 2)),
        dma((8, 2)), dma((8, 2)),
        dma((8,)), dma((8,)),
        dma((8,)), dma((8,)),
        dma((8,)), dma((8,)),
        dma((4,)), dma((4,)),
        pltpu.SemaphoreType.REGULAR((3,)),
    ]
    smem = pl.BlockSpec(memory_space=pltpu.SMEM)
    hbm = pl.BlockSpec(memory_space=pl.ANY)
    vmem = pl.BlockSpec(memory_space=pltpu.VMEM)
    return pl.pallas_call(
        kernel,
        out_shape=(
            vm((128, 256), BF16),
            vm((16, HD), BF16),
            vm((16, HD), BF16),
        ),
        in_specs=[smem, smem, hbm, hbm, hbm, hbm],
        out_specs=(vmem, vmem, vmem),
        scratch_shapes=scratch,
        compiler_params=pltpu.CompilerParams(
            collective_id=0, has_side_effects=True, vmem_limit_bytes=60 * 1024 * 1024
        ),
    )(
        doc_lengths,
        span_order.T,
        queries,
        out_grad,
        key_rows.reshape(4, 2, 16, HD),
        value_rows.reshape(4, 2, 16, HD),
    )


def solution(mesh):
    in_specs = (P("ctx", "head"), P("ctx", None), P("ctx", None), P("ctx", "head"), P(), P())
    out_specs = (P("ctx", "head"), P(("ctx", "head"), None), P(("ctx", "head"), None))
    return jax.shard_map(local, mesh=mesh, in_specs=in_specs, out_specs=out_specs, check_vma=False)
```

```python
import functools
import math

import jax
import jax.numpy as jnp
from jax import lax
from jax.experimental import pallas as pl
from jax.experimental.pallas import tpu as pltpu
from jax.sharding import PartitionSpec as P

MESH = pl.DeviceIdType.MESH
F32 = jnp.float32
BF16 = jnp.bfloat16
NU = 8
HD = 128
NEG = -1e30
SCALE = HD ** -0.5
EXP_SCALE = SCALE / math.log(2.0)
CK = 256
ROFF = (0, 1, 7, 2, 6, 3, 5, 4)
RPOS = {r: i for i, r in enumerate(ROFF)}
UQ = 256


def swap_rows(v, p):
    parts = [v[(k ^ p) * 2 : (k ^ p) * 2 + 2] for k in range(4)]
    return jnp.concatenate(parts, axis=0)


def kernel(
    lens_ref, order_ref, q_ref, g_ref, k_ref, v_ref,
    dq_ref, dk_ref, dv_ref,
    kv, qa, ga, qs, gs, kp, qlim, es, dps, ws, dss, dqa, pf, stm, st, rst, fac,
    dqb, dqr, sb, xr, yb, yr, zb, zr,
    lsem, qsend, qrecv, ysend, yrecv, xsend, xrecv, ssend, srecv, dsend, drecv,
    rsend, rrecv, rysend, ryrecv, zsend, zrecv, nearsem,
):
    ctx = lax.axis_index("ctx")
    head = lax.axis_index("head")
    zl, y, x = ctx // 32, (ctx // 4) % 8, ctx % 4
    zh, core = head // 2, head % 2
    xg = x + 1 - 2 * (x % 2)
    xo = (x + 3 + 2 * (x % 2)) % 4

    def at(zl_, y_, x_):
        return zl_ * 32 + y_ * 4 + x_

    odev = (at(zl, y, xo), head)
    ydev = [(at(zl, (y + r) % 8, x), head) for r in range(8)]
    zdev = [(ctx, ((zh + r) % 4) * 2 + core) for r in range(4)]
    gdev = [
        (
            at((zl + (k // 2) % 2) % 2, y, xg if k // 4 else x),
            zh * 2 + (core + k % 2) % 2,
        )
        for k in range(8)
    ]
    zout = (at(1 - zl, y, x), ((zh + 3 + 2 * zl) % 4) * 2 + core)

    stage = [
        pltpu.make_async_copy(k_ref.at[:, core], kv.at[0, 0, 0], lsem.at[0]),
        pltpu.make_async_copy(v_ref.at[:, core], kv.at[1, 0, 0], lsem.at[1]),
        pltpu.make_async_copy(q_ref, qa.at[0], lsem.at[2]),
        pltpu.make_async_copy(g_ref, ga.at[0], lsem.at[3]),
    ]
    for c in stage:
        c.start()

    def signal(sem, dev):
        pl.semaphore_signal(sem, inc=1, device_id=dev, device_id_type=MESH)

    barrier = pltpu.get_barrier_semaphore()
    peers = [odev, zout] + [ydev[r] for r in (1, 7, 2, 6, 3, 5)] + gdev[1:]
    for p in peers:
        signal(barrier, p)
    pl.semaphore_wait(barrier, len(peers))

    pending = []

    def send(src, dst, ss, rs, dev):
        c = pltpu.make_async_remote_copy(
            src_ref=src, dst_ref=dst, send_sem=ss, recv_sem=rs,
            device_id=dev, device_id_type=MESH,
        )
        c.start()
        pending.append(c)

    def landed(dst, ss, rs):
        pltpu.make_async_remote_copy(
            src_ref=dst, dst_ref=dst, send_sem=ss, recv_sem=rs,
            device_id=odev, device_id_type=MESH,
        ).wait_recv()

    def blk(c, r):
        return kv.at[:, RPOS[r % 8], c]

    def x_forward(r):
        r = r % 8
        send(blk(0, r), blk(1, r), xsend.at[r], xrecv.at[r], odev)

    def x_landed(r):
        r = r % 8
        landed(blk(1, r), xsend.at[r], xrecv.at[r])

    def y_send(r):
        send(blk(0, 0), blk(0, -r), ysend.at[r], yrecv.at[r], ydev[r])

    def y_landed(r):
        landed(blk(0, r), ysend.at[(-r) % 8], yrecv.at[(-r) % 8])

    def part(i, r):
        return kv.at[i, RPOS[r], 0]

    stage[0].wait()
    stage[1].wait()
    y_send(1)
    y_send(7)
    x_forward(0)
    for r in (2, 6, 3, 5):
        y_send(r)
    for k in (2, 4, 1):
        send(q_ref, qa.at[k], qsend.at[k, 0], qrecv.at[k, 0], gdev[k])
        send(g_ref, ga.at[k], qsend.at[k, 1], qrecv.at[k, 1], gdev[k])
    signal(nearsem.at[0], zout)
    signal(nearsem.at[1], gdev[2])

    lane = lax.broadcasted_iota(jnp.int32, (8, HD), 1) % 64
    starts = []
    total = jnp.int32(0)
    for i in range(8):
        starts.append(total)
        total = total + lens_ref[i]
    for g in range(4):
        octx = at((zl + g % 2) % 2, y, xg if g // 2 else x)
        for h in range(2):
            u = g * 2 + h
            qp = order_ref[h, octx] * 64 + lane
            first = jnp.zeros_like(qp)
            for s in starts:
                first = jnp.maximum(first, jnp.where(qp >= s, s, 0))
            qlim[u, 0] = qp
            qlim[u, 1] = first
    row = lax.broadcasted_iota(jnp.int32, (32, HD), 0)
    pattern = (row // 16) * 32 + row % 16 + core * 16
    for rp in range(8):
        for c in range(2):
            octx = at(zl, (y + ROFF[rp]) % 8, xo if c else x)
            for h in range(2):
                o = ((rp % 2) * 2 + c) * 64 + h * 32
                kp[rp // 2, o : o + 32, :] = pattern + order_ref[h, octx] * 64

    def units(g):
        for h in range(2):
            u = g * 2 + h
            for dc in range(2):
                for hd in range(2):
                    rows = slice(h * 64, h * 64 + 64)
                    cols = slice(hd * HD, hd * HD + HD)
                    o = (dc * 2 + hd) * 64
                    qs[u, o : o + 64, :] = qa[g * 2 + dc, rows, cols]
                    gs[u, o : o + 64, :] = ga[g * 2 + dc, rows, cols]

    def pass1(j, g):
        keys = kv[0, 2 * j : 2 * j + 2].reshape(CK, HD)
        vals = kv[1, 2 * j : 2 * j + 2].reshape(CK, HD)
        dims = (((1,), (1,)), ((), ()))
        for h in range(2):
            u = g * 2 + h
            s = lax.dot_general(keys, qs[u], dims, preferred_element_type=F32)
            dp = lax.dot_general(vals, gs[u], dims, preferred_element_type=F32)
            dps[j, u] = dp
            pos = kp[j]
            allowed = (pos <= qlim[u, 0, 0:1, :]) & (pos >= qlim[u, 1, 0:1, :])
            for dc in range(2):
                cols = slice(dc * HD, dc * HD + HD)
                row = (g * 2 + dc) * 2 + h
                sh = jnp.where(allowed, s[:, cols], NEG)
                m = jnp.max(sh, axis=0, keepdims=True)
                e = jnp.exp2((sh - m) * EXP_SCALE)
                es[j, u, :, cols] = e
                stm[j, 0, row : row + 1, :] = m
                stm[j, 1, row : row + 1, :] = jnp.sum(e, axis=0, keepdims=True)
                stm[j, 2, row : row + 1, :] = jnp.sum(e * dp[:, cols], axis=0, keepdims=True)

    def q_landed(k):
        landed(qa.at[k], qsend.at[k, 0], qrecv.at[k, 0])

    def g_landed(k):
        landed(ga.at[k], qsend.at[k, 1], qrecv.at[k, 1])

    def q_pass(k, to, dev):
        send(qa.at[k], qa.at[to], qsend.at[to, 0], qrecv.at[to, 0], dev)

    def g_pass(k, to, dev):
        send(ga.at[k], ga.at[to], qsend.at[to, 1], qrecv.at[to, 1], dev)

    stage[2].wait()
    stage[3].wait()
    q_landed(1)
    g_landed(1)
    units(0)
    y_landed(7)
    x_forward(7)
    y_landed(1)
    x_forward(1)
    y_landed(6)
    send(part(0, 6), part(0, 4), ysend.at[4], yrecv.at[4], ydev[2])
    x_forward(6)
    y_landed(2)
    send(part(1, 2), part(1, 4), ysend.at[0], yrecv.at[0], ydev[6])
    x_forward(2)
    q_landed(2)
    q_pass(2, 6, gdev[4])
    q_pass(2, 3, gdev[1])
    q_landed(4)
    q_pass(4, 5, gdev[1])
    g_landed(4)
    g_pass(4, 6, gdev[2])
    g_pass(4, 5, gdev[1])
    g_landed(2)
    g_pass(2, 3, gdev[1])
    x_landed(0)
    x_landed(1)
    pl.semaphore_wait(nearsem.at[0], 1)
    pl.semaphore_wait(nearsem.at[1], 1)
    signal(nearsem.at[2], zdev[3])
    pass1(0, 0)
    y_landed(5)
    x_forward(5)
    y_landed(3)
    x_forward(3)
    landed(part(0, 4), ysend.at[4], yrecv.at[4])
    landed(part(1, 4), ysend.at[0], yrecv.at[0])
    x_forward(4)
    q_landed(6)
    q_pass(6, 7, gdev[1])
    g_landed(6)
    g_pass(6, 7, gdev[1])
    q_landed(3)
    g_landed(3)
    units(1)
    pass1(0, 1)
    q_landed(5)
    g_landed(5)
    units(2)
    pass1(0, 2)
    x_landed(7)
    x_landed(2)
    pass1(1, 0)
    pass1(1, 1)
    pass1(1, 2)
    q_landed(7)
    g_landed(7)
    units(3)
    pass1(0, 3)
    pass1(1, 3)
    x_landed(6)
    x_landed(3)
    for g in range(4):
        pass1(2, g)
    x_landed(5)
    x_landed(4)
    def top(vals):
        while len(vals) > 1:
            vals = [jnp.maximum(a, b) for a, b in zip(vals[::2], vals[1::2])]
        return vals[0]

    def own_stats(dx):
        rows = slice(dx * 8, dx * 8 + 8)
        ms = [stm[j, 0, rows] for j in range(4)]
        m = top(ms)
        sc = [jnp.exp2((a - m) * EXP_SCALE) for a in ms]
        st[dx, 0] = m
        st[dx, 1] = sum(sc[j] * stm[j, 1, rows] for j in range(4))
        st[dx, 2] = sum(sc[j] * stm[j, 2, rows] for j in range(4))
        for k in (6, 7, 4, 5, 2, 3, 1):
            to = rst.at[k, (dx + k // 4) % 2]
            send(st.at[dx], to, ssend.at[k, dx], srecv.at[k, (dx + k // 4) % 2], gdev[k])

    pass1(3, 0)
    pass1(3, 1)
    own_stats(0)
    pass1(3, 2)
    pass1(3, 3)
    own_stats(1)
    pl.semaphore_wait(nearsem.at[2], 1)
    for dx in range(2):
        rows = slice(dx * 8, dx * 8 + 8)
        for k in range(1, 8):
            landed(rst.at[k, dx], ssend.at[k, dx], srecv.at[k, dx])
        got = [[st[dx, i]] + [swap_rows(rst[p, dx, i], p % 4) for p in range(1, 8)] for i in range(3)]
        gm = top(got[0])
        sc = [jnp.exp2((a - gm) * EXP_SCALE) for a in got[0]]
        inv = 1.0 / sum(sc[p] * got[1][p] for p in range(8))
        fac[4, rows] = sum(sc[p] * got[2][p] for p in range(8)) * inv
        for j in range(4):
            fac[j, rows] = jnp.exp2((stm[j, 0, rows] - gm) * EXP_SCALE) * inv

    def block(c, j0, nj, first):
        nk = nj * 128
        for u in range(NU):
            g, h = u // 2, u % 2
            for dc in range(2):
                row = (g * 2 + dc) * 2 + h
                cols = slice(dc * HD, dc * HD + HD)
                o = u * UQ + dc * HD
                delta = fac[4, row : row + 1, :]
                for i in range(2 * nj):
                    j = j0 + i // 2
                    ko = ((i % 2) * 2 + c) * 64
                    w = es[j, u, ko : ko + 64, cols] * fac[j, row : row + 1, :]
                    ws[i * 64 : i * 64 + 64, o : o + HD] = w.astype(BF16)
                    d = w * (dps[j, u, ko : ko + 64, cols] - delta)
                    dss[i * 64 : i * 64 + 64, o : o + HD] = d.astype(BF16)
        dims = (((1,), (0,)), ((), ()))
        q_all = qs[...].reshape(NU * UQ, HD)
        g_all = gs[...].reshape(NU * UQ, HD)
        r0, n = 2 * j0, 2 * nj
        dkc = lax.dot_general(dss[0:nk], q_all, dims, preferred_element_type=F32)
        pf[c, 0, r0 : r0 + n] = dkc.reshape(n, 64, HD)
        dvc = lax.dot_general(ws[0:nk], g_all, dims, preferred_element_type=F32)
        pf[c, 1, r0 : r0 + n] = dvc.reshape(n, 64, HD)
        keys = kv[0, r0 : r0 + n, c].reshape(nk, HD)
        add = lax.dot_general(
            dss[0:nk], keys, (((0,), (0,)), ((), ())), preferred_element_type=F32
        )
        if first:
            dqa[...] = add
        else:
            dqa[...] += add

    def mine(c, r):
        return pf[c, :, RPOS[r]]

    def x_send(r):
        sb[r] = mine(1, r).astype(BF16)
        send(sb.at[r], xr.at[r], rsend.at[r], rrecv.at[r], odev)

    def column_sum(r):
        landed(xr.at[r], rsend.at[r], rrecv.at[r])
        return mine(0, r) + xr[r].astype(F32)

    def y_out(r, to):
        send(yb.at[r], yr.at[r], rysend.at[r], ryrecv.at[r], ydev[to])

    def y_in(r):
        landed(yr.at[r], rysend.at[r], ryrecv.at[r])

    block(1, 3, 1, True)
    x_send(4)
    x_send(5)
    block(1, 2, 1, False)
    x_send(3)
    x_send(6)
    block(0, 2, 2, False)
    block(1, 0, 2, False)
    for r in (2, 1, 7, 0):
        x_send(r)
    yb[4] = column_sum(4).astype(BF16)
    send(yb.at[4, 0], yr.at[4, 0], rysend.at[4], ryrecv.at[4], ydev[2])
    send(yb.at[4, 1], yr.at[4, 1], rysend.at[0], ryrecv.at[0], ydev[6])
    block(0, 0, 2, False)
    yb[5] = column_sum(5).astype(BF16)
    y_out(5, 5)
    yb[3] = column_sum(3).astype(BF16)
    y_out(3, 3)

    def dq_part(k, h, hd):
        o = ((k // 2) * 2 + h) * UQ + ((k % 2) * 2 + hd) * 64
        return dqa[o : o + 64, :]

    for k in (6, 7, 4, 5, 2, 3, 1):
        for h in range(2):
            for hd in range(2):
                rows = slice(h * 64, h * 64 + 64)
                cols = slice(hd * HD, hd * HD + HD)
                dqb[k, rows, cols] = dq_part(k, h, hd).astype(BF16)
        send(dqb.at[k], dqr.at[k], dsend.at[k], drecv.at[k], gdev[k])

    t6 = column_sum(6)
    t2 = column_sum(2)
    landed(yr.at[4, 1], rysend.at[0], ryrecv.at[0])
    yb[6, 0] = t6[0].astype(BF16)
    yb[6, 1] = (t6[1] + yr[4, 1].astype(F32)).astype(BF16)
    y_out(6, 6)
    landed(yr.at[4, 0], rysend.at[4], ryrecv.at[4])
    yb[2, 0] = (t2[0] + yr[4, 0].astype(F32)).astype(BF16)
    yb[2, 1] = t2[1].astype(BF16)
    y_out(2, 2)
    yb[1] = column_sum(1).astype(BF16)
    y_out(1, 1)
    yb[7] = column_sum(7).astype(BF16)
    y_out(7, 7)
    own = column_sum(0)
    for r in (5, 3, 1, 6, 2, 7):
        y_in(r)
        own = own + yr[r].astype(F32)
    pf[0, :, 0] = own
    for r in (2, 1, 3):
        o = pl.multiple_of(((zh + r) % 4) * 16, 16)
        zb[r] = pf[0, :, 0, pl.ds(o, 16), :].astype(BF16)
        send(zb.at[r], zr.at[r], zsend.at[r], zrecv.at[r], zdev[r])
    fin = pf[0, :, 0, pl.ds(pl.multiple_of(zh * 16, 16), 16), :]
    for k in range(1, 8):
        landed(dqr.at[k], dsend.at[k], drecv.at[k])
    for h in range(2):
        for hd in range(2):
            rows = slice(h * 64, h * 64 + 64)
            cols = slice(hd * HD, hd * HD + HD)
            t = dq_part(0, h, hd)
            for k in range(1, 8):
                t = t + dqr[k, rows, cols].astype(F32)
            dq_ref[rows, cols] = (t * SCALE).astype(BF16)
    for c in pending:
        c.wait_send()
    for r in (1, 3, 2):
        landed(zr.at[r], zsend.at[r], zrecv.at[r])
        fin = fin + zr[r].astype(F32)
    dk_ref[...] = (fin[0] * SCALE).astype(BF16)
    dv_ref[...] = fin[1].astype(BF16)


def local(queries, key_rows, value_rows, out_grad, doc_lengths, span_order):
    vm = pltpu.VMEM
    dma = pltpu.SemaphoreType.DMA
    piece = (2, 64, HD)
    scratch = [
        vm((2, 8, 2, 4, 16, HD), BF16),
        vm((8, 128, 256), BF16),
        vm((8, 128, 256), BF16),
        vm((NU, UQ, HD), BF16),
        vm((NU, UQ, HD), BF16),
        vm((4, CK, HD), jnp.int32),
        vm((NU, 2, 8, HD), jnp.int32),
        vm((4, NU, CK, UQ), F32),
        vm((4, NU, CK, UQ), F32),
        vm((CK, NU * UQ), BF16),
        vm((CK, NU * UQ), BF16),
        vm((NU * UQ, HD), F32),
        vm((2, 2, 8, 64, HD), F32),
        vm((4, 3, 16, HD), F32),
        vm((2, 3, 8, HD), F32),
        vm((8, 2, 3, 8, HD), F32),
        vm((5, 16, HD), F32),
        vm((8, 128, 256), BF16),
        vm((8, 128, 256), BF16),
        vm((8,) + piece, BF16),
        vm((8,) + piece, BF16),
        vm((8,) + piece, BF16),
        vm((8,) + piece, BF16),
        vm((4, 2, 16, HD), BF16),
        vm((4, 2, 16, HD), BF16),
        dma((4,)),
        dma((8, 2)), dma((8, 2)),
        dma((8,)), dma((8,)),
        dma((8,)), dma((8,)),
        dma((8, 2)), dma((8, 2)),
        dma((8,)), dma((8,)),
        dma((8,)), dma((8,)),
        dma((8,)), dma((8,)),
        dma((4,)), dma((4,)),
        pltpu.SemaphoreType.REGULAR((3,)),
    ]
    smem = pl.BlockSpec(memory_space=pltpu.SMEM)
    hbm = pl.BlockSpec(memory_space=pl.ANY)
    vmem = pl.BlockSpec(memory_space=pltpu.VMEM)
    return pl.pallas_call(
        kernel,
        out_shape=(
            vm((128, 256), BF16),
            vm((16, HD), BF16),
            vm((16, HD), BF16),
        ),
        in_specs=[smem, smem, hbm, hbm, hbm, hbm],
        out_specs=(vmem, vmem, vmem),
        scratch_shapes=scratch,
        compiler_params=pltpu.CompilerParams(
            collective_id=0, has_side_effects=True, vmem_limit_bytes=60 * 1024 * 1024
        ),
    )(
        doc_lengths,
        span_order.T,
        queries,
        out_grad,
        key_rows.reshape(4, 2, 16, HD),
        value_rows.reshape(4, 2, 16, HD),
    )


def solution(mesh):
    in_specs = (P("ctx", "head"), P("ctx", None), P("ctx", None), P("ctx", "head"), P(), P())
    out_specs = (P("ctx", "head"), P(("ctx", "head"), None), P(("ctx", "head"), None))
    return jax.shard_map(local, mesh=mesh, in_specs=in_specs, out_specs=out_specs, check_vma=False)
```

```python
import functools
import math

import jax
import jax.numpy as jnp
from jax import lax
from jax.experimental import pallas as pl
from jax.experimental.pallas import tpu as pltpu
from jax.sharding import PartitionSpec as P

MESH = pl.DeviceIdType.MESH
F32 = jnp.float32
BF16 = jnp.bfloat16
NU = 8
HD = 128
NEG = -1e30
SCALE = HD ** -0.5
EXP_SCALE = SCALE / math.log(2.0)
CK = 256
ROFF = (0, 1, 7, 2, 6, 3, 5, 4)
RPOS = {r: i for i, r in enumerate(ROFF)}
UQ = 256


def swap_rows(v, p):
    if p == 0:
        return v
    parts = [v[(k ^ p) * 2 : (k ^ p) * 2 + 2] for k in range(4)]
    return jnp.concatenate(parts, axis=0)


def kernel(
    lens_ref, order_ref, q_ref, g_ref, k_ref, v_ref,
    dq_ref, dk_ref, dv_ref,
    kv, qa, ga, qs, gs, kp, qlim, es, dps, ws, dss, dqa, pf, stm, st, rst, fac,
    dqb, dqr, sb, xr, yb, yr, zb, zr,
    lsem, qsend, qrecv, ysend, yrecv, xsend, xrecv, ssend, srecv, dsend, drecv,
    rsend, rrecv, rysend, ryrecv, zsend, zrecv, nearsem,
):
    ctx = lax.axis_index("ctx")
    head = lax.axis_index("head")
    zl, y, x = ctx // 32, (ctx // 4) % 8, ctx % 4
    zh, core = head // 2, head % 2
    xg = x + 1 - 2 * (x % 2)
    xo = (x + 3 + 2 * (x % 2)) % 4

    def at(zl_, y_, x_):
        return zl_ * 32 + y_ * 4 + x_

    odev = (at(zl, y, xo), head)
    ydev = [(at(zl, (y + r) % 8, x), head) for r in range(8)]
    ddev = [(at(zl, (y + r) % 8, xo), head) for r in range(8)]
    zdev = [(ctx, ((zh + r) % 4) * 2 + core) for r in range(4)]
    gdev = [
        (
            at((zl + (k // 2) % 2) % 2, y, xg if k // 4 else x),
            zh * 2 + (core + k % 2) % 2,
        )
        for k in range(8)
    ]
    zout = (at(1 - zl, y, x), ((zh + 3 + 2 * zl) % 4) * 2 + core)

    stage = [
        pltpu.make_async_copy(k_ref.at[:, core], kv.at[0, 0, 0], lsem.at[0]),
        pltpu.make_async_copy(v_ref.at[:, core], kv.at[1, 0, 0], lsem.at[1]),
        pltpu.make_async_copy(q_ref, qa.at[0], lsem.at[2]),
        pltpu.make_async_copy(g_ref, ga.at[0], lsem.at[3]),
    ]
    for c in stage:
        c.start()

    def signal(sem, dev):
        pl.semaphore_signal(sem, inc=1, device_id=dev, device_id_type=MESH)

    barrier = pltpu.get_barrier_semaphore()
    peers = [odev, zout] + [ydev[r] for r in (1, 7, 2, 6, 3, 5)] + gdev[1:]
    peers = peers + [ddev[r] for r in (1, 7, 2, 6)]
    for p in peers:
        signal(barrier, p)
    pl.semaphore_wait(barrier, len(peers))

    pending = []

    def send(src, dst, ss, rs, dev):
        c = pltpu.make_async_remote_copy(
            src_ref=src, dst_ref=dst, send_sem=ss, recv_sem=rs,
            device_id=dev, device_id_type=MESH,
        )
        c.start()
        pending.append(c)

    def landed(dst, ss, rs):
        pltpu.make_async_remote_copy(
            src_ref=dst, dst_ref=dst, send_sem=ss, recv_sem=rs,
            device_id=odev, device_id_type=MESH,
        ).wait_recv()

    def blk(c, r):
        return kv.at[:, RPOS[r % 8], c]

    def x_forward(r):
        r = r % 8
        send(blk(0, r), blk(1, r), xsend.at[r], xrecv.at[r], odev)

    def x_landed(r):
        r = r % 8
        landed(blk(1, r), xsend.at[r], xrecv.at[r])

    def y_send(r):
        send(blk(0, 0), blk(0, -r), ysend.at[r], yrecv.at[r], ydev[r])

    def y_landed(i, r):
        landed(blk(0, r), ysend.at[i], yrecv.at[i])

    def part(i, r, c=0):
        return kv.at[i, RPOS[r], c]

    stage[0].wait()
    stage[1].wait()
    y_send(1)
    y_send(7)
    x_forward(0)
    y_send(2)
    y_send(6)
    for k in (2, 4, 1):
        send(q_ref, qa.at[k], qsend.at[k, 0], qrecv.at[k, 0], gdev[k])
        send(g_ref, ga.at[k], qsend.at[k, 1], qrecv.at[k, 1], gdev[k])
    signal(nearsem.at[0], zout)
    signal(nearsem.at[1], gdev[2])

    lane = lax.broadcasted_iota(jnp.int32, (8, HD), 1) % 64
    starts = []
    total = jnp.int32(0)
    for i in range(8):
        starts.append(total)
        total = total + lens_ref[i]
    for g in range(4):
        octx = at((zl + g % 2) % 2, y, xg if g // 2 else x)
        for h in range(2):
            u = g * 2 + h
            qp = order_ref[h, octx] * 64 + lane
            first = jnp.zeros_like(qp)
            for s in starts:
                first = jnp.maximum(first, jnp.where(qp >= s, s, 0))
            qlim[u, 0] = qp
            qlim[u, 1] = first
    row = lax.broadcasted_iota(jnp.int32, (32, HD), 0)
    pattern = (row // 16) * 32 + row % 16 + core * 16
    for rp in range(8):
        for c in range(2):
            octx = at(zl, (y + ROFF[rp]) % 8, xo if c else x)
            for h in range(2):
                o = ((rp % 2) * 2 + c) * 64 + h * 32
                kp[rp // 2, o : o + 32, :] = pattern + order_ref[h, octx] * 64

    def units(g):
        for h in range(2):
            u = g * 2 + h
            for dc in range(2):
                for hd in range(2):
                    rows = slice(h * 64, h * 64 + 64)
                    cols = slice(hd * HD, hd * HD + HD)
                    o = (dc * 2 + hd) * 64
                    qs[u, o : o + 64, :] = qa[g * 2 + dc, rows, cols]
                    gs[u, o : o + 64, :] = ga[g * 2 + dc, rows, cols]

    def pass1(j, g):
        keys = kv[0, 2 * j : 2 * j + 2].reshape(CK, HD)
        vals = kv[1, 2 * j : 2 * j + 2].reshape(CK, HD)
        dims = (((1,), (1,)), ((), ()))
        for h in range(2):
            u = g * 2 + h
            s = lax.dot_general(keys, qs[u], dims, preferred_element_type=F32)
            dp = lax.dot_general(vals, gs[u], dims, preferred_element_type=F32)
            dps[j, u] = dp
            pos = kp[j]
            allowed = (pos <= qlim[u, 0, 0:1, :]) & (pos >= qlim[u, 1, 0:1, :])
            for dc in range(2):
                cols = slice(dc * HD, dc * HD + HD)
                row = (g * 2 + dc) * 2 + h
                sh = jnp.where(allowed, s[:, cols], NEG)
                m = jnp.max(sh, axis=0, keepdims=True)
                e = jnp.exp2((sh - m) * EXP_SCALE)
                es[j, u, :, cols] = e
                stm[j, 0, row : row + 1, :] = m
                stm[j, 1, row : row + 1, :] = jnp.sum(e, axis=0, keepdims=True)
                stm[j, 2, row : row + 1, :] = jnp.sum(e * dp[:, cols], axis=0, keepdims=True)

    def q_landed(k):
        landed(qa.at[k], qsend.at[k, 0], qrecv.at[k, 0])

    def g_landed(k):
        landed(ga.at[k], qsend.at[k, 1], qrecv.at[k, 1])

    def q_pass(k, to, dev):
        send(qa.at[k], qa.at[to], qsend.at[to, 0], qrecv.at[to, 0], dev)

    def g_pass(k, to, dev):
        send(ga.at[k], ga.at[to], qsend.at[to, 1], qrecv.at[to, 1], dev)

    stage[2].wait()
    stage[3].wait()
    q_landed(1)
    g_landed(1)
    units(0)
    y_landed(1, 7)
    x_forward(7)
    y_landed(7, 1)
    x_forward(1)
    y_landed(2, 6)
    send(blk(0, 6), blk(0, 5), ysend.at[3], yrecv.at[3], ydev[1])
    send(part(0, 6), part(0, 4), ysend.at[4], yrecv.at[4], ydev[2])
    x_forward(6)
    send(blk(0, 6), blk(1, 5), xsend.at[5], xrecv.at[5], ddev[1])
    send(part(0, 6), part(0, 4, 1), xsend.at[4], xrecv.at[4], ddev[2])
    y_landed(6, 2)
    send(blk(0, 2), blk(0, 3), ysend.at[5], yrecv.at[5], ydev[7])
    send(part(1, 2), part(1, 4), ysend.at[0], yrecv.at[0], ydev[6])
    x_forward(2)
    send(blk(0, 2), blk(1, 3), xsend.at[3], xrecv.at[3], ddev[7])
    send(part(1, 2), part(1, 4, 1), xsend.at[8], xrecv.at[8], ddev[6])
    q_landed(2)
    q_pass(2, 6, gdev[4])
    q_pass(2, 3, gdev[1])
    q_landed(4)
    q_pass(4, 5, gdev[1])
    g_landed(4)
    g_pass(4, 6, gdev[2])
    g_pass(4, 5, gdev[1])
    g_landed(2)
    g_pass(2, 3, gdev[1])
    x_landed(0)
    x_landed(1)
    pl.semaphore_wait(nearsem.at[0], 1)
    pl.semaphore_wait(nearsem.at[1], 1)
    signal(nearsem.at[2], zdev[3])
    pass1(0, 0)
    y_landed(3, 5)
    y_landed(5, 3)
    landed(part(0, 4), ysend.at[4], yrecv.at[4])
    landed(part(1, 4), ysend.at[0], yrecv.at[0])
    q_landed(6)
    q_pass(6, 7, gdev[1])
    g_landed(6)
    g_pass(6, 7, gdev[1])
    q_landed(3)
    g_landed(3)
    units(1)
    pass1(0, 1)
    q_landed(5)
    g_landed(5)
    units(2)
    pass1(0, 2)
    x_landed(7)
    x_landed(2)
    pass1(1, 0)
    pass1(1, 1)
    pass1(1, 2)
    q_landed(7)
    g_landed(7)
    units(3)
    pass1(0, 3)
    pass1(1, 3)
    x_landed(6)
    x_landed(3)
    for g in range(4):
        pass1(2, g)
    x_landed(5)
    landed(part(0, 4, 1), xsend.at[4], xrecv.at[4])
    landed(part(1, 4, 1), xsend.at[8], xrecv.at[8])
    def top(vals):
        while len(vals) > 1:
            vals = [jnp.maximum(a, b) for a, b in zip(vals[::2], vals[1::2])]
        return vals[0]

    def own_stats(dx):
        rows = slice(dx * 8, dx * 8 + 8)
        ms = [stm[j, 0, rows] for j in range(4)]
        m = top(ms)
        sc = [jnp.exp2((a - m) * EXP_SCALE) for a in ms]
        st[dx, 0] = m
        st[dx, 1] = sum(sc[j] * stm[j, 1, rows] for j in range(4))
        st[dx, 2] = sum(sc[j] * stm[j, 2, rows] for j in range(4))
        for k in (6, 7, 4, 5, 2, 3, 1):
            to = rst.at[k, (dx + k // 4) % 2]
            send(st.at[dx], to, ssend.at[k, dx], srecv.at[k, (dx + k // 4) % 2], gdev[k])

    pass1(3, 0)
    pass1(3, 1)
    own_stats(0)
    pass1(3, 2)
    pass1(3, 3)
    own_stats(1)
    pl.semaphore_wait(nearsem.at[2], 1)
    for dx in range(2):
        rows = slice(dx * 8, dx * 8 + 8)
        for k in range(1, 8):
            landed(rst.at[k, dx], ssend.at[k, dx], srecv.at[k, dx])
        got = [[st[dx, i]] + [rst[p, dx, i] for p in range(1, 8)] for i in range(3)]
        gm = top([swap_rows(jnp.maximum(got[0][p], got[0][p + 4]), p) for p in range(4)])
        total, dot = None, None
        for p in range(4):
            back = swap_rows(gm, p)
            a = jnp.exp2((got[0][p] - back) * EXP_SCALE)
            b = jnp.exp2((got[0][p + 4] - back) * EXP_SCALE)
            l = swap_rows(a * got[1][p] + b * got[1][p + 4], p)
            d = swap_rows(a * got[2][p] + b * got[2][p + 4], p)
            total = l if total is None else total + l
            dot = d if dot is None else dot + d
        inv = 1.0 / total
        fac[4, rows] = dot * inv
        for j in range(4):
            fac[j, rows] = jnp.exp2((stm[j, 0, rows] - gm) * EXP_SCALE) * inv

    def elements(c, j0, nj):
        for u in range(NU):
            g, h = u // 2, u % 2
            for dc in range(2):
                row = (g * 2 + dc) * 2 + h
                cols = slice(dc * HD, dc * HD + HD)
                o = u * UQ + dc * HD
                delta = fac[4, row : row + 1, :]
                for i in range(2 * nj):
                    j = j0 + i // 2
                    ko = ((i % 2) * 2 + c) * 64
                    w = es[j, u, ko : ko + 64, cols] * fac[j, row : row + 1, :]
                    ws[i * 64 : i * 64 + 64, o : o + HD] = w.astype(BF16)
                    d = w * (dps[j, u, ko : ko + 64, cols] - delta)
                    ro = j0 * 128 + i * 64
                    dss[c, ro : ro + 64, o : o + HD] = d.astype(BF16)

    def key_part(c, j0, nj):
        dims = (((1,), (0,)), ((), ()))
        q_all = qs[...].reshape(NU * UQ, HD)
        g_all = gs[...].reshape(NU * UQ, HD)
        nk, r0, n = nj * 128, 2 * j0, 2 * nj
        ko = j0 * 128
        dkc = lax.dot_general(dss[c, ko : ko + nk], q_all, dims, preferred_element_type=F32)
        pf[c, 0, r0 : r0 + n] = dkc.reshape(n, 64, HD)
        dvc = lax.dot_general(ws[0:nk], g_all, dims, preferred_element_type=F32)
        pf[c, 1, r0 : r0 + n] = dvc.reshape(n, 64, HD)

    def query_part(g):
        dims = (((0,), (0,)), ((), ()))
        o = g * 2 * UQ
        t = None
        for c in range(2):
            keys = kv[0, :, c].reshape(512, HD)
            a = lax.dot_general(
                dss[c, :, o : o + 2 * UQ], keys, dims, preferred_element_type=F32
            )
            t = a if t is None else t + a
        dqa[...] = t
        for dc in range(2):
            k = g * 2 + dc
            if k > 0:
                for h in range(2):
                    for hd in range(2):
                        rows = slice(h * 64, h * 64 + 64)
                        cols = slice(hd * HD, hd * HD + HD)
                        a = h * UQ + (dc * 2 + hd) * 64
                        dqb[k, rows, cols] = dqa[a : a + 64, :].astype(BF16)
                send(dqb.at[k], dqr.at[k], dsend.at[k], drecv.at[k], gdev[k])

    def mine(c, r):
        return pf[c, :, RPOS[r]]

    def x_send(r):
        sb[r] = mine(1, r).astype(BF16)
        send(sb.at[r], xr.at[r], rsend.at[r], rrecv.at[r], odev)

    def column_sum(r):
        landed(xr.at[r], rsend.at[r], rrecv.at[r])
        return mine(0, r) + xr[r].astype(F32)

    def y_out(r, to):
        send(yb.at[r], yr.at[r], rysend.at[r], ryrecv.at[r], ydev[to])

    def y_in(r):
        landed(yr.at[r], rysend.at[r], ryrecv.at[r])

    elements(1, 3, 1)
    key_part(1, 3, 1)
    x_send(4)
    x_send(5)
    elements(1, 2, 1)
    key_part(1, 2, 1)
    x_send(3)
    x_send(6)
    elements(1, 0, 2)
    key_part(1, 0, 2)
    for r in (2, 1, 7, 0):
        x_send(r)
    elements(0, 2, 2)
    key_part(0, 2, 2)
    yb[4] = column_sum(4).astype(BF16)
    send(yb.at[4, 0], yr.at[4, 0], rysend.at[4], ryrecv.at[4], ydev[2])
    send(yb.at[4, 1], yr.at[4, 1], rysend.at[0], ryrecv.at[0], ydev[6])
    elements(0, 0, 2)
    query_part(3)
    query_part(2)
    yb[5] = column_sum(5).astype(BF16)
    y_out(5, 5)
    yb[3] = column_sum(3).astype(BF16)
    y_out(3, 3)
    query_part(1)
    query_part(0)
    key_part(0, 0, 2)

    t6 = column_sum(6)
    t2 = column_sum(2)
    landed(yr.at[4, 1], rysend.at[0], ryrecv.at[0])
    yb[6, 0] = t6[0].astype(BF16)
    yb[6, 1] = (t6[1] + yr[4, 1].astype(F32)).astype(BF16)
    y_out(6, 6)
    landed(yr.at[4, 0], rysend.at[4], ryrecv.at[4])
    yb[2, 0] = (t2[0] + yr[4, 0].astype(F32)).astype(BF16)
    yb[2, 1] = t2[1].astype(BF16)
    y_out(2, 2)
    yb[1] = column_sum(1).astype(BF16)
    y_out(1, 1)
    yb[7] = column_sum(7).astype(BF16)
    y_out(7, 7)
    own = column_sum(0)
    for r in (5, 3, 1, 6, 2, 7):
        y_in(r)
        own = own + yr[r].astype(F32)
    pf[0, :, 0] = own
    for r in (2, 1, 3):
        o = pl.multiple_of(((zh + r) % 4) * 16, 16)
        zb[r] = pf[0, :, 0, pl.ds(o, 16), :].astype(BF16)
        send(zb.at[r], zr.at[r], zsend.at[r], zrecv.at[r], zdev[r])
    fin = pf[0, :, 0, pl.ds(pl.multiple_of(zh * 16, 16), 16), :]
    for k in range(1, 8):
        landed(dqr.at[k], dsend.at[k], drecv.at[k])
    for h in range(2):
        for hd in range(2):
            rows = slice(h * 64, h * 64 + 64)
            cols = slice(hd * HD, hd * HD + HD)
            o = h * UQ + hd * 64
            t = dqa[o : o + 64, :]
            for k in range(1, 8):
                t = t + dqr[k, rows, cols].astype(F32)
            dq_ref[rows, cols] = (t * SCALE).astype(BF16)
    for c in pending:
        c.wait_send()
    for r in (1, 3, 2):
        landed(zr.at[r], zsend.at[r], zrecv.at[r])
        fin = fin + zr[r].astype(F32)
    dk_ref[...] = (fin[0] * SCALE).astype(BF16)
    dv_ref[...] = fin[1].astype(BF16)


def local(queries, key_rows, value_rows, out_grad, doc_lengths, span_order):
    vm = pltpu.VMEM
    dma = pltpu.SemaphoreType.DMA
    piece = (2, 64, HD)
    scratch = [
        vm((2, 8, 2, 4, 16, HD), BF16),
        vm((8, 128, 256), BF16),
        vm((8, 128, 256), BF16),
        vm((NU, UQ, HD), BF16),
        vm((NU, UQ, HD), BF16),
        vm((4, CK, HD), jnp.int32),
        vm((NU, 2, 8, HD), jnp.int32),
        vm((4, NU, CK, UQ), F32),
        vm((4, NU, CK, UQ), F32),
        vm((CK, NU * UQ), BF16),
        vm((2, 512, NU * UQ), BF16),
        vm((2 * UQ, HD), F32),
        vm((2, 2, 8, 64, HD), F32),
        vm((4, 3, 16, HD), F32),
        vm((2, 3, 8, HD), F32),
        vm((8, 2, 3, 8, HD), F32),
        vm((5, 16, HD), F32),
        vm((8, 128, 256), BF16),
        vm((8, 128, 256), BF16),
        vm((8,) + piece, BF16),
        vm((8,) + piece, BF16),
        vm((8,) + piece, BF16),
        vm((8,) + piece, BF16),
        vm((4, 2, 16, HD), BF16),
        vm((4, 2, 16, HD), BF16),
        dma((4,)),
        dma((8, 2)), dma((8, 2)),
        dma((8,)), dma((8,)),
        dma((9,)), dma((9,)),
        dma((8, 2)), dma((8, 2)),
        dma((8,)), dma((8,)),
        dma((8,)), dma((8,)),
        dma((8,)), dma((8,)),
        dma((4,)), dma((4,)),
        pltpu.SemaphoreType.REGULAR((3,)),
    ]
    smem = pl.BlockSpec(memory_space=pltpu.SMEM)
    hbm = pl.BlockSpec(memory_space=pl.ANY)
    vmem = pl.BlockSpec(memory_space=pltpu.VMEM)
    return pl.pallas_call(
        kernel,
        out_shape=(
            vm((128, 256), BF16),
            vm((16, HD), BF16),
            vm((16, HD), BF16),
        ),
        in_specs=[smem, smem, hbm, hbm, hbm, hbm],
        out_specs=(vmem, vmem, vmem),
        scratch_shapes=scratch,
        compiler_params=pltpu.CompilerParams(
            collective_id=0, has_side_effects=True, vmem_limit_bytes=60 * 1024 * 1024
        ),
    )(
        doc_lengths,
        span_order.T,
        queries,
        out_grad,
        key_rows.reshape(4, 2, 16, HD),
        value_rows.reshape(4, 2, 16, HD),
    )


def solution(mesh):
    in_specs = (P("ctx", "head"), P("ctx", None), P("ctx", None), P("ctx", "head"), P(), P())
    out_specs = (P("ctx", "head"), P(("ctx", "head"), None), P(("ctx", "head"), None))
    return jax.shard_map(local, mesh=mesh, in_specs=in_specs, out_specs=out_specs, check_vma=False)
```

```python
import functools
import math

import jax
import jax.numpy as jnp
from jax import lax
from jax.experimental import pallas as pl
from jax.experimental.pallas import tpu as pltpu
from jax.sharding import PartitionSpec as P

MESH = pl.DeviceIdType.MESH
F32 = jnp.float32
BF16 = jnp.bfloat16
NU = 8
HD = 128
NEG = -1e30
SCALE = HD ** -0.5
EXP_SCALE = SCALE / math.log(2.0)
CK = 256
ROFF = (0, 1, 7, 2, 6, 3, 5, 4)
RPOS = {r: i for i, r in enumerate(ROFF)}
UQ = 256


def swap_rows(v, p):
    if p == 0:
        return v
    parts = [v[(k ^ p) * 2 : (k ^ p) * 2 + 2] for k in range(4)]
    return jnp.concatenate(parts, axis=0)


def kernel(
    lens_ref, order_ref, q_ref, g_ref, k_ref, v_ref,
    dq_ref, dk_ref, dv_ref,
    kv, qa, ga, qs, gs, kp, qlim, es, dps, ws, dss, dqa, pf, stm, st, rst, fac,
    dqb, dqr, sb, xr, yb, yr, zb, zr,
    lsem, qsend, qrecv, ysend, yrecv, xsend, xrecv, ssend, srecv, dsend, drecv,
    rsend, rrecv, rysend, ryrecv, zsend, zrecv, nearsem,
):
    ctx = lax.axis_index("ctx")
    head = lax.axis_index("head")
    zl, y, x = ctx // 32, (ctx // 4) % 8, ctx % 4
    zh, core = head // 2, head % 2
    xg = x + 1 - 2 * (x % 2)
    xo = (x + 3 + 2 * (x % 2)) % 4

    def at(zl_, y_, x_):
        return zl_ * 32 + y_ * 4 + x_

    odev = (at(zl, y, xo), head)
    ydev = [(at(zl, (y + r) % 8, x), head) for r in range(8)]
    ddev = [(at(zl, (y + r) % 8, xo), head) for r in range(8)]
    zdev = [(ctx, ((zh + r) % 4) * 2 + core) for r in range(4)]
    gdev = [
        (
            at((zl + (k // 2) % 2) % 2, y, xg if k // 4 else x),
            zh * 2 + (core + k % 2) % 2,
        )
        for k in range(8)
    ]
    zout = (at(1 - zl, y, x), ((zh + 3 + 2 * zl) % 4) * 2 + core)

    stage = [
        pltpu.make_async_copy(k_ref.at[:, core], kv.at[0, 0, 0], lsem.at[0]),
        pltpu.make_async_copy(v_ref.at[:, core], kv.at[1, 0, 0], lsem.at[1]),
        pltpu.make_async_copy(q_ref, qa.at[0], lsem.at[2]),
        pltpu.make_async_copy(g_ref, ga.at[0], lsem.at[3]),
    ]
    for c in stage:
        c.start()

    def signal(sem, dev):
        pl.semaphore_signal(sem, inc=1, device_id=dev, device_id_type=MESH)

    barrier = pltpu.get_barrier_semaphore()
    peers = [odev, zout] + [ydev[r] for r in (1, 7, 2, 6, 3, 5)] + gdev[1:]
    peers = peers + [ddev[r] for r in (1, 7, 2, 6)]
    for p in peers:
        signal(barrier, p)
    pl.semaphore_wait(barrier, len(peers))

    pending = []

    def send(src, dst, ss, rs, dev):
        c = pltpu.make_async_remote_copy(
            src_ref=src, dst_ref=dst, send_sem=ss, recv_sem=rs,
            device_id=dev, device_id_type=MESH,
        )
        c.start()
        pending.append(c)

    def landed(dst, ss, rs):
        pltpu.make_async_remote_copy(
            src_ref=dst, dst_ref=dst, send_sem=ss, recv_sem=rs,
            device_id=odev, device_id_type=MESH,
        ).wait_recv()

    def blk(c, r):
        return kv.at[:, RPOS[r % 8], c]

    def x_forward(r):
        r = r % 8
        send(blk(0, r), blk(1, r), xsend.at[r], xrecv.at[r], odev)

    def x_landed(r):
        r = r % 8
        landed(blk(1, r), xsend.at[r], xrecv.at[r])

    def y_send(r):
        send(blk(0, 0), blk(0, -r), ysend.at[r], yrecv.at[r], ydev[r])

    def y_landed(i, r):
        landed(blk(0, r), ysend.at[i], yrecv.at[i])

    def part(i, r, c=0):
        return kv.at[i, RPOS[r], c]

    stage[0].wait()
    stage[1].wait()
    y_send(1)
    y_send(7)
    x_forward(0)
    y_send(2)
    y_send(6)
    for k in (2, 4, 1):
        send(q_ref, qa.at[k], qsend.at[k, 0], qrecv.at[k, 0], gdev[k])
        send(g_ref, ga.at[k], qsend.at[k, 1], qrecv.at[k, 1], gdev[k])
    signal(nearsem.at[0], zout)
    signal(nearsem.at[1], gdev[2])

    lane = lax.broadcasted_iota(jnp.int32, (8, HD), 1) % 64
    starts = []
    total = jnp.int32(0)
    for i in range(8):
        starts.append(total)
        total = total + lens_ref[i]
    for g in range(4):
        octx = at((zl + g % 2) % 2, y, xg if g // 2 else x)
        for h in range(2):
            u = g * 2 + h
            qp = order_ref[h, octx] * 64 + lane
            first = jnp.zeros_like(qp)
            for s in starts:
                first = jnp.maximum(first, jnp.where(qp >= s, s, 0))
            qlim[u, 0] = qp
            qlim[u, 1] = first
    row = lax.broadcasted_iota(jnp.int32, (32, HD), 0)
    pattern = (row // 16) * 32 + row % 16 + core * 16
    for rp in range(8):
        for c in range(2):
            octx = at(zl, (y + ROFF[rp]) % 8, xo if c else x)
            for h in range(2):
                o = ((rp % 2) * 2 + c) * 64 + h * 32
                kp[rp // 2, o : o + 32, :] = pattern + order_ref[h, octx] * 64

    def units(g):
        for h in range(2):
            u = g * 2 + h
            for dc in range(2):
                for hd in range(2):
                    rows = slice(h * 64, h * 64 + 64)
                    cols = slice(hd * HD, hd * HD + HD)
                    o = (dc * 2 + hd) * 64
                    qs[u, o : o + 64, :] = qa[g * 2 + dc, rows, cols]
                    gs[u, o : o + 64, :] = ga[g * 2 + dc, rows, cols]

    def pass1(j, g):
        keys = kv[0, 2 * j : 2 * j + 2].reshape(CK, HD)
        vals = kv[1, 2 * j : 2 * j + 2].reshape(CK, HD)
        dims = (((1,), (1,)), ((), ()))
        for h in range(2):
            u = g * 2 + h
            s = lax.dot_general(keys, qs[u], dims, preferred_element_type=F32)
            dp = lax.dot_general(vals, gs[u], dims, preferred_element_type=F32)
            dps[j, u] = dp
            pos = kp[j]
            allowed = (pos <= qlim[u, 0, 0:1, :]) & (pos >= qlim[u, 1, 0:1, :])
            for dc in range(2):
                cols = slice(dc * HD, dc * HD + HD)
                row = (g * 2 + dc) * 2 + h
                sh = jnp.where(allowed, s[:, cols], NEG)
                m = jnp.max(sh, axis=0, keepdims=True)
                e = jnp.exp2((sh - m) * EXP_SCALE)
                es[j, u, :, cols] = e
                stm[j, 0, row : row + 1, :] = m
                stm[j, 1, row : row + 1, :] = jnp.sum(e, axis=0, keepdims=True)
                stm[j, 2, row : row + 1, :] = jnp.sum(e * dp[:, cols], axis=0, keepdims=True)

    def q_landed(k):
        landed(qa.at[k], qsend.at[k, 0], qrecv.at[k, 0])

    def g_landed(k):
        landed(ga.at[k], qsend.at[k, 1], qrecv.at[k, 1])

    def q_pass(k, to, dev):
        send(qa.at[k], qa.at[to], qsend.at[to, 0], qrecv.at[to, 0], dev)

    def g_pass(k, to, dev):
        send(ga.at[k], ga.at[to], qsend.at[to, 1], qrecv.at[to, 1], dev)

    y_landed(1, 7)
    x_forward(7)
    y_landed(7, 1)
    x_forward(1)
    y_landed(2, 6)
    send(blk(0, 6), blk(0, 5), ysend.at[3], yrecv.at[3], ydev[1])
    send(part(0, 6), part(0, 4), ysend.at[4], yrecv.at[4], ydev[2])
    x_forward(6)
    send(blk(0, 6), blk(1, 5), xsend.at[5], xrecv.at[5], ddev[1])
    send(part(0, 6), part(0, 4, 1), xsend.at[4], xrecv.at[4], ddev[2])
    y_landed(6, 2)
    send(blk(0, 2), blk(0, 3), ysend.at[5], yrecv.at[5], ydev[7])
    send(part(1, 2), part(1, 4), ysend.at[0], yrecv.at[0], ydev[6])
    x_forward(2)
    send(blk(0, 2), blk(1, 3), xsend.at[3], xrecv.at[3], ddev[7])
    send(part(1, 2), part(1, 4, 1), xsend.at[8], xrecv.at[8], ddev[6])
    q_landed(2)
    q_pass(2, 6, gdev[4])
    q_pass(2, 3, gdev[1])
    q_landed(4)
    q_pass(4, 5, gdev[1])
    g_landed(4)
    g_pass(4, 6, gdev[2])
    g_pass(4, 5, gdev[1])
    g_landed(2)
    g_pass(2, 3, gdev[1])
    stage[2].wait()
    stage[3].wait()
    q_landed(1)
    g_landed(1)
    units(0)
    x_landed(0)
    x_landed(1)
    pl.semaphore_wait(nearsem.at[0], 1)
    pl.semaphore_wait(nearsem.at[1], 1)
    signal(nearsem.at[2], zdev[3])
    pass1(0, 0)
    y_landed(3, 5)
    y_landed(5, 3)
    landed(part(0, 4), ysend.at[4], yrecv.at[4])
    landed(part(1, 4), ysend.at[0], yrecv.at[0])
    q_landed(6)
    q_pass(6, 7, gdev[1])
    g_landed(6)
    g_pass(6, 7, gdev[1])
    q_landed(3)
    g_landed(3)
    units(1)
    pass1(0, 1)
    q_landed(5)
    g_landed(5)
    units(2)
    pass1(0, 2)
    x_landed(7)
    x_landed(2)
    pass1(1, 0)
    pass1(1, 1)
    pass1(1, 2)
    q_landed(7)
    g_landed(7)
    units(3)
    pass1(0, 3)
    pass1(1, 3)
    x_landed(6)
    x_landed(3)
    for g in range(4):
        pass1(2, g)
    x_landed(5)
    landed(part(0, 4, 1), xsend.at[4], xrecv.at[4])
    landed(part(1, 4, 1), xsend.at[8], xrecv.at[8])
    def top(vals):
        while len(vals) > 1:
            vals = [jnp.maximum(a, b) for a, b in zip(vals[::2], vals[1::2])]
        return vals[0]

    def own_stats(dx):
        rows = slice(dx * 8, dx * 8 + 8)
        ms = [stm[j, 0, rows] for j in range(4)]
        m = top(ms)
        sc = [jnp.exp2((a - m) * EXP_SCALE) for a in ms]
        st[dx, 0] = m
        st[dx, 1] = sum(sc[j] * stm[j, 1, rows] for j in range(4))
        st[dx, 2] = sum(sc[j] * stm[j, 2, rows] for j in range(4))
        for k in (6, 7, 4, 5, 2, 3, 1):
            to = rst.at[k, (dx + k // 4) % 2]
            send(st.at[dx], to, ssend.at[k, dx], srecv.at[k, (dx + k // 4) % 2], gdev[k])

    pass1(3, 0)
    pass1(3, 1)
    own_stats(0)
    pass1(3, 2)
    pass1(3, 3)
    own_stats(1)
    pl.semaphore_wait(nearsem.at[2], 1)
    for dx in range(2):
        rows = slice(dx * 8, dx * 8 + 8)
        for k in range(1, 8):
            landed(rst.at[k, dx], ssend.at[k, dx], srecv.at[k, dx])
        got = [[st[dx, i]] + [rst[p, dx, i] for p in range(1, 8)] for i in range(3)]
        gm = top([swap_rows(jnp.maximum(got[0][p], got[0][p + 4]), p) for p in range(4)])
        total, dot = None, None
        for p in range(4):
            back = swap_rows(gm, p)
            a = jnp.exp2((got[0][p] - back) * EXP_SCALE)
            b = jnp.exp2((got[0][p + 4] - back) * EXP_SCALE)
            l = swap_rows(a * got[1][p] + b * got[1][p + 4], p)
            d = swap_rows(a * got[2][p] + b * got[2][p + 4], p)
            total = l if total is None else total + l
            dot = d if dot is None else dot + d
        inv = 1.0 / total
        fac[4, rows] = dot * inv
        for j in range(4):
            fac[j, rows] = jnp.exp2((stm[j, 0, rows] - gm) * EXP_SCALE) * inv

    def elements(c, j0, nj):
        for u in range(NU):
            g, h = u // 2, u % 2
            for dc in range(2):
                row = (g * 2 + dc) * 2 + h
                cols = slice(dc * HD, dc * HD + HD)
                o = u * UQ + dc * HD
                delta = fac[4, row : row + 1, :]
                for i in range(2 * nj):
                    j = j0 + i // 2
                    ko = ((i % 2) * 2 + c) * 64
                    w = es[j, u, ko : ko + 64, cols] * fac[j, row : row + 1, :]
                    ws[i * 64 : i * 64 + 64, o : o + HD] = w.astype(BF16)
                    d = w * (dps[j, u, ko : ko + 64, cols] - delta)
                    ro = j0 * 128 + i * 64
                    dss[c, ro : ro + 64, o : o + HD] = d.astype(BF16)

    def key_part(c, j0, nj):
        dims = (((1,), (0,)), ((), ()))
        q_all = qs[...].reshape(NU * UQ, HD)
        g_all = gs[...].reshape(NU * UQ, HD)
        nk, r0, n = nj * 128, 2 * j0, 2 * nj
        ko = j0 * 128
        dkc = lax.dot_general(dss[c, ko : ko + nk], q_all, dims, preferred_element_type=F32)
        pf[c, 0, r0 : r0 + n] = dkc.reshape(n, 64, HD)
        dvc = lax.dot_general(ws[0:nk], g_all, dims, preferred_element_type=F32)
        pf[c, 1, r0 : r0 + n] = dvc.reshape(n, 64, HD)

    def query_part(g):
        dims = (((0,), (0,)), ((), ()))
        o = g * 2 * UQ
        t = None
        for c in range(2):
            keys = kv[0, :, c].reshape(512, HD)
            a = lax.dot_general(
                dss[c, :, o : o + 2 * UQ], keys, dims, preferred_element_type=F32
            )
            t = a if t is None else t + a
        dqa[...] = t
        for dc in range(2):
            k = g * 2 + dc
            if k > 0:
                for h in range(2):
                    for hd in range(2):
                        rows = slice(h * 64, h * 64 + 64)
                        cols = slice(hd * HD, hd * HD + HD)
                        a = h * UQ + (dc * 2 + hd) * 64
                        dqb[k, rows, cols] = dqa[a : a + 64, :].astype(BF16)
                send(dqb.at[k], dqr.at[k], dsend.at[k], drecv.at[k], gdev[k])

    def mine(c, r):
        return pf[c, :, RPOS[r]]

    def x_send(r):
        sb[r] = mine(1, r).astype(BF16)
        send(sb.at[r], xr.at[r], rsend.at[r], rrecv.at[r], odev)

    def column_sum(r):
        landed(xr.at[r], rsend.at[r], rrecv.at[r])
        return mine(0, r) + xr[r].astype(F32)

    def y_out(r, to):
        send(yb.at[r], yr.at[r], rysend.at[r], ryrecv.at[r], ydev[to])

    def y_in(r):
        landed(yr.at[r], rysend.at[r], ryrecv.at[r])

    elements(1, 3, 1)
    key_part(1, 3, 1)
    x_send(4)
    x_send(5)
    elements(1, 2, 1)
    key_part(1, 2, 1)
    x_send(3)
    x_send(6)
    elements(1, 0, 2)
    key_part(1, 0, 2)
    for r in (2, 1, 7, 0):
        x_send(r)
    elements(0, 2, 2)
    key_part(0, 2, 2)
    yb[4] = column_sum(4).astype(BF16)
    send(yb.at[4, 0], yr.at[4, 0], rysend.at[4], ryrecv.at[4], ydev[2])
    send(yb.at[4, 1], yr.at[4, 1], rysend.at[0], ryrecv.at[0], ydev[6])
    elements(0, 0, 2)
    query_part(3)
    query_part(2)
    yb[5] = column_sum(5).astype(BF16)
    y_out(5, 5)
    yb[3] = column_sum(3).astype(BF16)
    y_out(3, 3)
    query_part(1)
    query_part(0)
    key_part(0, 0, 2)

    t6 = column_sum(6)
    t2 = column_sum(2)
    landed(yr.at[4, 1], rysend.at[0], ryrecv.at[0])
    yb[6, 0] = t6[0].astype(BF16)
    yb[6, 1] = (t6[1] + yr[4, 1].astype(F32)).astype(BF16)
    y_out(6, 6)
    landed(yr.at[4, 0], rysend.at[4], ryrecv.at[4])
    yb[2, 0] = (t2[0] + yr[4, 0].astype(F32)).astype(BF16)
    yb[2, 1] = t2[1].astype(BF16)
    y_out(2, 2)
    yb[1] = column_sum(1).astype(BF16)
    y_out(1, 1)
    yb[7] = column_sum(7).astype(BF16)
    y_out(7, 7)
    own = column_sum(0)
    for r in (5, 3, 1, 6, 2, 7):
        y_in(r)
        own = own + yr[r].astype(F32)
    pf[0, :, 0] = own
    for r in (2, 1, 3):
        o = pl.multiple_of(((zh + r) % 4) * 16, 16)
        zb[r] = pf[0, :, 0, pl.ds(o, 16), :].astype(BF16)
        send(zb.at[r], zr.at[r], zsend.at[r], zrecv.at[r], zdev[r])
    fin = pf[0, :, 0, pl.ds(pl.multiple_of(zh * 16, 16), 16), :]
    for k in range(1, 8):
        landed(dqr.at[k], dsend.at[k], drecv.at[k])
    for h in range(2):
        for hd in range(2):
            rows = slice(h * 64, h * 64 + 64)
            cols = slice(hd * HD, hd * HD + HD)
            o = h * UQ + hd * 64
            t = dqa[o : o + 64, :]
            for k in range(1, 8):
                t = t + dqr[k, rows, cols].astype(F32)
            dq_ref[rows, cols] = (t * SCALE).astype(BF16)
    for c in pending:
        c.wait_send()
    for r in (1, 3, 2):
        landed(zr.at[r], zsend.at[r], zrecv.at[r])
        fin = fin + zr[r].astype(F32)
    dk_ref[...] = (fin[0] * SCALE).astype(BF16)
    dv_ref[...] = fin[1].astype(BF16)


def local(queries, key_rows, value_rows, out_grad, doc_lengths, span_order):
    vm = pltpu.VMEM
    dma = pltpu.SemaphoreType.DMA
    piece = (2, 64, HD)
    scratch = [
        vm((2, 8, 2, 4, 16, HD), BF16),
        vm((8, 128, 256), BF16),
        vm((8, 128, 256), BF16),
        vm((NU, UQ, HD), BF16),
        vm((NU, UQ, HD), BF16),
        vm((4, CK, HD), jnp.int32),
        vm((NU, 2, 8, HD), jnp.int32),
        vm((4, NU, CK, UQ), F32),
        vm((4, NU, CK, UQ), F32),
        vm((CK, NU * UQ), BF16),
        vm((2, 512, NU * UQ), BF16),
        vm((2 * UQ, HD), F32),
        vm((2, 2, 8, 64, HD), F32),
        vm((4, 3, 16, HD), F32),
        vm((2, 3, 8, HD), F32),
        vm((8, 2, 3, 8, HD), F32),
        vm((5, 16, HD), F32),
        vm((8, 128, 256), BF16),
        vm((8, 128, 256), BF16),
        vm((8,) + piece, BF16),
        vm((8,) + piece, BF16),
        vm((8,) + piece, BF16),
        vm((8,) + piece, BF16),
        vm((4, 2, 16, HD), BF16),
        vm((4, 2, 16, HD), BF16),
        dma((4,)),
        dma((8, 2)), dma((8, 2)),
        dma((8,)), dma((8,)),
        dma((9,)), dma((9,)),
        dma((8, 2)), dma((8, 2)),
        dma((8,)), dma((8,)),
        dma((8,)), dma((8,)),
        dma((8,)), dma((8,)),
        dma((4,)), dma((4,)),
        pltpu.SemaphoreType.REGULAR((3,)),
    ]
    smem = pl.BlockSpec(memory_space=pltpu.SMEM)
    hbm = pl.BlockSpec(memory_space=pl.ANY)
    vmem = pl.BlockSpec(memory_space=pltpu.VMEM)
    return pl.pallas_call(
        kernel,
        out_shape=(
            vm((128, 256), BF16),
            vm((16, HD), BF16),
            vm((16, HD), BF16),
        ),
        in_specs=[smem, smem, hbm, hbm, hbm, hbm],
        out_specs=(vmem, vmem, vmem),
        scratch_shapes=scratch,
        compiler_params=pltpu.CompilerParams(
            collective_id=0, has_side_effects=True, vmem_limit_bytes=60 * 1024 * 1024
        ),
    )(
        doc_lengths,
        span_order.T,
        queries,
        out_grad,
        key_rows.reshape(4, 2, 16, HD),
        value_rows.reshape(4, 2, 16, HD),
    )


def solution(mesh):
    in_specs = (P("ctx", "head"), P("ctx", None), P("ctx", None), P("ctx", "head"), P(), P())
    out_specs = (P("ctx", "head"), P(("ctx", "head"), None), P(("ctx", "head"), None))
    return jax.shard_map(local, mesh=mesh, in_specs=in_specs, out_specs=out_specs, check_vma=False)
```
